512 devices in a mesh: level: 16 (over z_hi, y, core), dom: 32 (over z_lo, x).
Axes of the slice: x: 4, y: 4, z: 16 (z_hi: 2, z_lo: 8; z = z_hi * 8 + z_lo), core: 2. Of those that a mesh axis runs over, the one named last changes fastest.
Arguments:
- right_side: float32 [128, 256, 128], P('dom', 'level'), may hold values from -6 to 6
- fine_blocks: float32 [128, 8, 128, 128], P('dom'), may hold values from -0.06 to 0.06
- fine_cols: int32 [128, 8], P('dom'), may hold values from 0 to 7, as said below
- fine_edges: int32 [64], P('dom'), may hold values from 0 to 3, as said below
- mid_blocks: float32 [64, 8, 128, 128], P('dom'), may hold values from -0.06 to 0.06
- mid_cols: int32 [64, 8], P('dom'), may hold values from 0 to 3, as said below
- mid_edges: int32 [32], P('dom'), may hold values from 0 to 1, as said below
- fine_map: int32 [128], P('dom'), may hold values from 0 to 1, as said below
- mid_map: int32 [64], P('dom'), may hold values from 0 to 7, as said below
- coarse_inverse: float32 [1024, 1024], P('level'), may hold values from -0.1875 to 0.1875
Outputs:
- solution: float32 [128, 256, 128], P('dom', 'level')
The draws below stay inside these ranges and needn't reach their ends.
Inputs may be any that keep to these rules, and one draw needn't show every extreme that they name: `fine_cols`: slot 0 of every block row is the row itself; each row refers to a boundary row of its lower and of its upper partition where these exist, and never past the first or last partition; slots may repeat. `fine_edges`: distinct within each partition. `mid_cols`: slot 0 of every block row is the row itself; each row refers to a boundary row of its lower and of its upper partition where these exist, and never past the first or last partition; slots may repeat. `mid_edges`: distinct within each partition. `fine_map`: each middle block row of a partition receives exactly two of its fine block rows. `mid_map`: each coarse block row receives exactly 8 middle block rows, from any partitions.
All inputs are finite; a program needn't handle non-finite values.
Results may differ from the reference program's by a relative error of at most 0.0003.
Values sent between devices are 32-bit elements; how exact they have to be, the bound alone decides.
A program may use at most 64 MiB of HBM per device.

```python
import jax
import jax.numpy as jnp
from jax import lax

B = 128
NNZ = 8
NNZ_M = 8
BND = 2
BND_M = 1
ROWS_DEV = 4
CAGG = 8
DEG = 4
ITERS = 1
MID_DEV = 2
NBR = 128
NMR = 64
CRB = 8
NRHS = 256


def pattern(key, row_count, slot_count, edge_count, part_count):
    key_list = jax.random.split(key, 4)
    edge_lists = jax.vmap(lambda sub_key: jax.random.permutation(sub_key, row_count)[:edge_count])(jax.random.split(key_list[0], part_count)).astype(jnp.int32)
    edge_lists = edge_lists.at[0].set(jnp.arange(row_count - edge_count, row_count, dtype=jnp.int32))
    edge_lists = edge_lists.at[1].set(jnp.arange(edge_count, dtype=jnp.int32))
    row_total = row_count * part_count
    owner_part = jnp.arange(row_total, dtype=jnp.int32) // row_count
    local_row = jnp.arange(row_total, dtype=jnp.int32) % row_count
    kind_table = jax.random.randint(key_list[1], (row_total, slot_count), 0, 3).astype(jnp.int32)
    kind_table = kind_table.at[:, 1].set(1).at[:, 2].set(2)
    first_part = (owner_part == 0)[:, None]
    last_part = (owner_part == part_count - 1)[:, None]
    kind_table = jnp.where(first_part & (kind_table == 1), 2, kind_table)
    kind_table = jnp.where(last_part & (kind_table == 2), 1, kind_table)
    own_pick = jax.random.randint(key_list[2], (row_total, slot_count), 0, row_count).astype(jnp.int32)
    edge_pick = jax.random.randint(key_list[3], (row_total, slot_count), 0, edge_count).astype(jnp.int32)
    edge_pick = edge_pick.at[:, 1].set(local_row % edge_count).at[:, 2].set(local_row % edge_count)
    slot_table = jnp.where(kind_table == 0, own_pick, jnp.where(kind_table == 1, row_count + edge_pick, row_count + edge_count + edge_pick))
    slot_table = slot_table.at[:, 0].set(local_row)
    return (slot_table.astype(jnp.int32), edge_lists.reshape(-1).astype(jnp.int32))


def draw_fine_cols(key, part):
    return pattern(jax.random.fold_in(key, 11), ROWS_DEV, NNZ, BND, NBR // ROWS_DEV)[0]


def draw_fine_edges(key, part):
    return pattern(jax.random.fold_in(key, 11), ROWS_DEV, NNZ, BND, NBR // ROWS_DEV)[1]


def draw_mid_cols(key, part):
    return pattern(jax.random.fold_in(key, 12), MID_DEV, NNZ_M, BND_M, NMR // MID_DEV)[0]


def draw_mid_edges(key, part):
    return pattern(jax.random.fold_in(key, 12), MID_DEV, NNZ_M, BND_M, NMR // MID_DEV)[1]


def draw_fine_map(key, part):
    sub_keys = jax.random.split(jax.random.fold_in(key, 21), NBR // ROWS_DEV)
    mapped = jax.vmap(lambda sub_key: jax.random.permutation(sub_key, ROWS_DEV) % MID_DEV)(sub_keys)
    return mapped.reshape(-1).astype(jnp.int32)


def draw_mid_map(key, part):
    return (jax.random.permutation(jax.random.fold_in(key, 22), NMR) % CRB).astype(jnp.int32)


def block_scale(own_key, shape, cuts, smallest, largest):
    def one(position, parts):
        heights = jax.random.uniform(jax.random.fold_in(jax.random.fold_in(own_key, 6), position), (parts,), jnp.float32, smallest / len(cuts), largest / len(cuts))
        return jnp.repeat(jnp.exp(heights), shape[position] // parts).reshape((-1,) + (1,) * (len(shape) - position - 1))

    factor_of = one(*cuts[0])
    for cut in cuts[1:]:
        factor_of = factor_of * one(*cut)
    return factor_of


def normal_values(stream_key, shape, spread, reach, pieces=(), kind=jnp.bfloat16):
    values = jax.random.normal(stream_key, shape, jnp.float32) * spread
    if len(pieces) > 0:
        values = block_scale(stream_key, shape, pieces, -0.22, 0.18) * values
    return jnp.clip(values, min=-reach, max=reach).astype(kind)


def setup_inputs(seed: int = 0) -> dict:
    keys = jax.random.split(jax.random.key(seed), 11)
    return {
        "right_side": normal_values(keys[0], (NBR, NRHS, B), 1.0, 6.0, ((0, 32), (1, 16)), jnp.float32),
        "fine_blocks": normal_values(keys[1], (NBR, NNZ, B, B), 0.009, 0.06, ((0, 32),), jnp.float32),
        "fine_cols": draw_fine_cols(jax.random.fold_in(keys[10], 71), 0),
        "fine_edges": draw_fine_edges(jax.random.fold_in(keys[10], 71), 0),
        "mid_blocks": normal_values(keys[4], (NMR, NNZ_M, B, B), 0.009, 0.06, ((0, 32),), jnp.float32),
        "mid_cols": draw_mid_cols(jax.random.fold_in(keys[10], 71), 0),
        "mid_edges": draw_mid_edges(jax.random.fold_in(keys[10], 71), 0),
        "fine_map": draw_fine_map(jax.random.fold_in(keys[10], 71), 0),
        "mid_map": draw_mid_map(jax.random.fold_in(keys[10], 71), 0),
        "coarse_inverse": normal_values(keys[9], (CRB * B, CRB * B), (CRB * B) ** -0.5, 0.1875, ((0, 16),), jnp.float32),
    }


CENTRE = 1.0
HALF_WIDTH = 0.7
DAMPING = 0.7
MID_WEIGHT = 0.5 ** 0.5


def columns(col_local, edge_list, row_count, edge_count):
    part_count = col_local.shape[0] // row_count
    owner_part = (jnp.arange(col_local.shape[0], dtype=jnp.int32) // row_count)[:, None]
    below_part = jnp.clip(owner_part - 1, 0, part_count - 1)
    above_part = jnp.clip(owner_part + 1, 0, part_count - 1)
    own_col = owner_part * row_count + col_local
    below_col = below_part * row_count + edge_list[below_part * edge_count + jnp.clip(col_local - row_count, 0, edge_count - 1)]
    above_col = above_part * row_count + edge_list[above_part * edge_count + jnp.clip(col_local - row_count - edge_count, 0, edge_count - 1)]
    picked = jnp.where(col_local < row_count, own_col, jnp.where(col_local < row_count + edge_count, below_col, above_col))
    return picked.astype(jnp.int32)


def apply_level(blocks, col_global, values):
    picked = values[col_global]
    return values + jnp.einsum('rkab,rkvb->rva', blocks, picked, precision=lax.Precision.HIGHEST)


def smooth(apply_fn, source):
    sigma_ratio = CENTRE / HALF_WIDTH
    rho_prev = 1.0 / sigma_ratio
    step_dir = source / CENTRE
    result = step_dir
    for sweep_index in range(DEG - 1):
        rho_next = 1.0 / (2.0 * sigma_ratio - rho_prev)
        step_dir = (rho_next * rho_prev) * step_dir + (2.0 * rho_next / HALF_WIDTH) * (source - apply_fn(result))
        result = result + step_dir
        rho_prev = rho_next
    return result


def reference(right_side, fine_blocks, fine_cols, fine_edges, mid_blocks, mid_cols, mid_edges, fine_map, mid_map, coarse_inverse):
    fine_global = columns(fine_cols, fine_edges, ROWS_DEV, BND)
    mid_global = columns(mid_cols, mid_edges, MID_DEV, BND_M)

    def fine_apply(values):
        return apply_level(fine_blocks, fine_global, values)

    def mid_apply(values):
        return apply_level(mid_blocks, mid_global, values)

    parent = ((jnp.arange(NBR, dtype=jnp.int32) // ROWS_DEV) * MID_DEV + fine_map).astype(jnp.int32)
    coarse_weight = CAGG ** -0.5
    inverse_view = coarse_inverse.reshape(CRB * B, CRB, B)
    solution = jnp.zeros(right_side.shape, jnp.float32)
    for iteration in range(ITERS):
        if iteration == 0:
            residual = right_side
        else:
            residual = right_side - fine_apply(solution)
        fine_corr = smooth(fine_apply, residual)
        mid_res = MID_WEIGHT * jax.ops.segment_sum(residual, parent, NMR)
        mid_corr = smooth(mid_apply, mid_res)
        coarse_res = coarse_weight * jax.ops.segment_sum(mid_res, mid_map, CRB)
        coarse_flat = jnp.einsum('ocb,cvb->ov', inverse_view, coarse_res, precision=lax.Precision.HIGHEST)
        coarse_corr = coarse_flat.reshape(CRB, B, NRHS).transpose(0, 2, 1)
        joined = mid_corr + coarse_weight * coarse_corr[mid_map]
        solution = solution + DAMPING * (fine_corr + MID_WEIGHT * joined[parent])
    return solution
```

```python
import jax
import jax.numpy as jnp
from jax import lax
from jax.experimental import pallas as pl
from jax.experimental.pallas import tpu as pltpu
from jax.sharding import PartitionSpec as P

CAGG = 8
DEG = 4
CENTRE = 1.0
HALF_WIDTH = 0.7
DAMPING = 0.7
MID_WEIGHT = 0.5**0.5
COARSE_WEIGHT = CAGG**-0.5

F32 = jnp.float32
BF16 = jnp.bfloat16


def sweep_constants():
    ratio = CENTRE / HALF_WIDTH
    rho_prev = 1.0 / ratio
    constants = []
    for _ in range(DEG - 1):
        rho_next = 1.0 / (2.0 * ratio - rho_prev)
        constants.append((rho_next * rho_prev, 2.0 * rho_next / HALF_WIDTH))
        rho_prev = rho_next
    return constants


def split(value):
    high = value.astype(BF16)
    low = (value - high.astype(F32)).astype(BF16)
    return high, low


def product(left, right):
    full = lax.dot_general(left, right, (((1,), (1,)), ((), ())), preferred_element_type=F32)
    return full[:16, :128] + (full[:16, 128:] + full[16:, :128])


def wait_for(ref, sem):
    pltpu.make_async_copy(ref, ref, sem).wait()


def kernel(
    fine_cols,
    fine_edges,
    mid_cols,
    mid_edges,
    fine_map,
    mid_map,
    source_hbm,
    fine_hbm,
    mid_hbm,
    inverse_hbm,
    out,
    source,
    fine_raw,
    mid_raw,
    fine_w,
    mid_w,
    fine_e,
    fine_d,
    mid_g,
    mid_e,
    mid_d,
    fine_x,
    mid_x,
    halo_out,
    halo_in,
    raw_out,
    raw_in,
    res_out,
    res_in,
    inv_in,
    inv_w,
    corr_out,
    corr_in,
    final,
    picked,
    joined,
    load_sem,
    halo_send,
    halo_recv,
    raw_send,
    raw_recv,
    inv_send,
    inv_recv,
    res_send,
    res_recv,
    corr_send,
    corr_recv,
    z_send,
    z_recv,
    x_send,
    x_recv,
):
    level = lax.axis_index("level")
    dom = lax.axis_index("dom")
    half = level // 8
    mine = level % 8
    y_pos = mine // 2
    core = level % 2
    z_pos = dom // 4
    x_pos = dom % 4
    centre = (z_pos == 3) | (z_pos == 4)
    centre_i = jnp.where(centre, 1, 0)
    z_two = jnp.where(z_pos == 4, 1, 0)
    has_low = dom > 0
    has_high = dom < 31
    import_z = jnp.where(z_pos == 7, 3, 4)
    imports = (z_pos == 0) | (z_pos == 7)

    def remote(src, dst, send, recv, to_level, to_dom):
        return pltpu.make_async_remote_copy(
            src_ref=src,
            dst_ref=dst,
            send_sem=send,
            recv_sem=recv,
            device_id=(to_level, to_dom),
            device_id_type=pl.DeviceIdType.MESH,
        )

    load_source = pltpu.make_async_copy(source_hbm, source, load_sem.at[0])
    load_source.start()
    load_fine = [
        pltpu.make_async_copy(fine_hbm.at[r], fine_raw.at[r], load_sem.at[1 + r]) for r in range(4)
    ]
    load_mid = [
        pltpu.make_async_copy(mid_hbm.at[r], mid_raw.at[r], load_sem.at[5 + r]) for r in range(2)
    ]
    for load in load_fine + load_mid:
        load.start()

    barrier = pltpu.get_barrier_semaphore()

    def greet(to_level, to_dom):
        pl.semaphore_signal(
            barrier, inc=1, device_id=(to_level, to_dom), device_id_type=pl.DeviceIdType.MESH
        )

    @pl.when(has_low)
    def _():
        greet(level, dom - 1)

    @pl.when(has_high)
    def _():
        greet(level, dom + 1)

    for other_z in (3, 4):

        @pl.when(z_pos != other_z)
        def _():
            greet(level, other_z * 4 + x_pos)

    for step in range(1, 4):
        greet(level, z_pos * 4 + (x_pos + step) % 4)

    @pl.when(centre)
    def _():
        @pl.loop(1, 32)
        def _(step):
            greet(level, (dom + step) % 32)

        @pl.loop(1, 8)
        def _(step):
            greet(half * 8 + (mine + step) % 8, dom)

        @pl.when(core == 0)
        def _():
            greet(level + 1, dom)

        @pl.when(core == 1)
        def _():
            from_dom = jnp.where(z_pos == 3, 7, 0) * 4 + x_pos
            greet((1 - half) * 8 + y_pos * 2, from_dom)
            greet((1 - half) * 8 + y_pos * 2 + 1, from_dom)

    load_source.wait()
    lanes = lax.broadcasted_iota(jnp.int32, (1, 128), 1)
    for j in range(2):
        total = None
        for i in range(4):
            term = jnp.where(fine_map[i] == j, source[i], 0.0)
            total = term if total is None else total + term
        mid_g[j] = MID_WEIGHT * total
    raw_out[:, 6:8, :] = jnp.zeros((8, 2, 128), F32)
    for j in range(2):
        row = jnp.where((lanes < 16) & (lanes % 8 == mid_map[j]), 1.0, 0.0)
        for n in range(8):
            first = 4 * (n % 4) + 2 * (n // 4)
            raw_out[n, 2 * j : 2 * j + 2, :] = mid_g[j, first : first + 2, :]
            raw_out[n, 4 + j : 5 + j, :] = row

    def fill_halo(turn, fine_ref, mid_ref):
        halo_out[turn, 0] = fine_ref[fine_edges[0]]
        halo_out[turn, 1] = fine_ref[fine_edges[1]]
        halo_out[turn, 2] = mid_ref[mid_edges[0]]

    fill_halo(0, source, mid_g)

    @pl.when(dom == 0)
    def _():
        for turn in range(3):
            halo_in[turn, 0] = jnp.zeros((3, 16, 128), F32)

    @pl.when(dom == 31)
    def _():
        for turn in range(3):
            halo_in[turn, 1] = jnp.zeros((3, 16, 128), F32)

    sides = jnp.where(has_low, 1, 0) + jnp.where(has_high, 1, 0)
    waits = sides + 8 - centre_i + 3 + 14 * centre_i
    waits = waits + jnp.where(imports, 1, 0) + centre_i * core
    pl.semaphore_wait(barrier, waits)

    def halo_low(turn):
        return remote(
            halo_out.at[turn],
            halo_in.at[turn, 1],
            halo_send.at[turn, 0],
            halo_recv.at[turn, 1],
            level,
            dom - 1,
        )

    def halo_high(turn):
        return remote(
            halo_out.at[turn],
            halo_in.at[turn, 0],
            halo_send.at[turn, 1],
            halo_recv.at[turn, 0],
            level,
            dom + 1,
        )

    def start_halo(turn):
        @pl.when(has_low)
        def _():
            halo_low(turn).start()

        @pl.when(has_high)
        def _():
            halo_high(turn).start()

    def wait_halo(turn):
        @pl.when(has_low)
        def _():
            wait_for(halo_in.at[turn, 0], halo_recv.at[turn, 0])

        @pl.when(has_high)
        def _():
            wait_for(halo_in.at[turn, 1], halo_recv.at[turn, 1])

    start_halo(0)

    @pl.loop(0, 8)
    def _(n):
        to_dom = (3 + n // 4) * 4 + n % 4

        @pl.when(to_dom != dom)
        def _():
            remote(raw_out.at[n], raw_in.at[dom], raw_send, raw_recv, level, to_dom).start()

        @pl.when(to_dom == dom)
        def _():
            pltpu.make_async_copy(raw_out.at[n], raw_in.at[dom], raw_recv).start()

    @pl.when(centre & (core == 0))
    def _():
        pltpu.make_async_copy(inverse_hbm, inv_in.at[0], inv_recv).start()

    @pl.when(centre & (core == 1))
    def _():
        remote(inverse_hbm, inv_in.at[1], inv_send, inv_recv, level - 1, dom).start()

    @pl.when(imports)
    def _():
        remote(
            inverse_hbm,
            inv_in.at[core],
            inv_send,
            inv_recv,
            (1 - half) * 8 + y_pos * 2 + 1,
            import_z * 4 + x_pos,
        ).start()

    for r in range(4):
        load_fine[r].wait()
        for k in range(8):
            high, low = split(fine_raw[r, k])
            fine_w[r, 0:128, k * 128 : k * 128 + 128] = high
            fine_w[r, 128:256, k * 128 : k * 128 + 128] = low
    for r in range(2):
        load_mid[r].wait()
        for k in range(8):
            high, low = split(mid_raw[r, k])
            mid_w[r, 0:128, k * 128 : k * 128 + 128] = high
            mid_w[r, 128:256, k * 128 : k * 128 + 128] = low

    def put(ref, slot, value):
        high, low = split(value)
        ref[slot, 0:16, :] = high
        ref[slot, 16:32, :] = low

    constants = sweep_constants()

    def sweep(turn):
        keep, push = constants[turn]
        old_fine = source if turn == 0 else fine_e
        old_mid = mid_g if turn == 0 else mid_e
        old_fine_d = source if turn == 0 else fine_d
        old_mid_d = mid_g if turn == 0 else mid_d
        for r in range(4):
            put(fine_x, r, old_fine[r])
        for r in range(2):
            put(mid_x, r, old_mid[r])
        wait_halo(turn)
        for side in range(2):
            for row in range(2):
                put(fine_x, 4 + 2 * side + row, halo_in[turn, side, row])
            put(mid_x, 2 + side, halo_in[turn, side, 2])
        for r in range(4):
            left = jnp.concatenate([fine_x[fine_cols[r, k]] for k in range(8)], axis=1)
            applied = old_fine[r] + product(left, fine_w[r])
            step = keep * old_fine_d[r] + push * (source[r] - applied)
            fine_d[r] = step
            fine_e[r] = old_fine[r] + step
        for r in range(2):
            left = jnp.concatenate([mid_x[mid_cols[r, k]] for k in range(8)], axis=1)
            applied = old_mid[r] + product(left, mid_w[r])
            step = keep * old_mid_d[r] + push * (mid_g[r] - applied)
            mid_d[r] = step
            mid_e[r] = old_mid[r] + step
        if turn < 2:
            fill_halo(turn + 1, fine_e, mid_e)
            start_halo(turn + 1)

    sweep(0)

    @pl.when(centre)
    def _():
        wait_for(raw_in, raw_recv)
        rows = lax.broadcasted_iota(jnp.int32, (32, 8, 128), 1)
        cols = lax.broadcasted_iota(jnp.int32, (32, 8, 128), 2)
        value = raw_in[...]
        first = jnp.broadcast_to(value[:, 4:5, :], (32, 8, 128))
        second = jnp.broadcast_to(value[:, 5:6, :], (32, 8, 128))
        picks = jnp.where(rows < 2, first, second)
        wanted = (rows < 4) & (cols // 8 == rows % 2)
        picks = jnp.where(wanted, picks, 0.0).reshape(256, 128).astype(BF16)
        high, low = split(value.reshape(256, 128))
        both = jnp.concatenate([high, low], axis=1)
        full = lax.dot_general(picks, both, (((0,), (0,)), ((), ())), preferred_element_type=F32)
        total = full[:16, :128] + full[:16, 128:]
        res_out[...] = total

        @pl.loop(0, 8)
        def _(peer):
            @pl.when(peer != mine)
            def _():
                remote(res_out, res_in.at[mine], res_send, res_recv, half * 8 + peer, dom).start()

            @pl.when(peer == mine)
            def _():
                pltpu.make_async_copy(res_out, res_in.at[mine], res_recv).start()

    sweep(1)

    @pl.when(centre)
    def _():
        wait_for(inv_in, inv_recv)
        for h in range(2):
            high, low = split(inv_in[h])
            inv_w[64 * h : 64 * h + 64, :] = high
            inv_w[128 + 64 * h : 192 + 64 * h, :] = low
        wait_for(res_in, res_recv)
        parts = []
        for c in range(8):
            block = jnp.concatenate([res_in[:, c, :], res_in[:, 8 + c, :]], axis=0)
            high, low = split(block)
            parts.append(jnp.concatenate([high, low], axis=0))
        left = jnp.concatenate(parts, axis=1)
        corr = product(left, inv_w[...])
        for peer in range(8):
            corr_out[peer, 0:1, :] = corr[peer : peer + 1, :]
            corr_out[peer, 1:2, :] = corr[8 + peer : 9 + peer, :]
        row = jnp.where(core == 0, half, 1 - half) * 4 + y_pos

        @pl.loop(0, 8)
        def _(peer):
            @pl.when(peer != mine)
            def _():
                remote(
                    corr_out.at[peer], corr_in.at[row], corr_send, corr_recv, half * 8 + peer, dom
                ).start()

            @pl.when(peer == mine)
            def _():
                pltpu.make_async_copy(corr_out.at[peer], corr_in.at[row], corr_recv).start()

    sweep(2)

    @pl.when(centre)
    def _():
        wait_for(corr_in, corr_recv)

        @pl.loop(0, 8)
        def _(other_z):
            @pl.when(other_z != z_pos)
            def _():
                remote(
                    corr_in,
                    final.at[x_pos, z_two],
                    z_send,
                    z_recv,
                    level,
                    other_z * 4 + x_pos,
                ).start()

            @pl.when(other_z == z_pos)
            def _():
                pltpu.make_async_copy(corr_in, final.at[x_pos, z_two], z_recv).start()

    wait_for(final.at[0], z_recv)

    for step in range(1, 4):
        remote(
            final.at[x_pos],
            final.at[x_pos],
            x_send,
            x_recv,
            level,
            z_pos * 4 + (x_pos + step) % 4,
        ).start()
    wait_for(final.at[pl.ds(0, 3)], x_recv)

    for j in range(2):
        for n in range(8):
            first = 4 * (n // 2) + 2 * (n % 2)
            picked[first : first + 2, :] = final[n // 2, n % 2, mid_map[j]]
        joined[j] = mid_e[j] + (COARSE_WEIGHT * COARSE_WEIGHT) * picked[...]
    for i in range(4):
        out[i] = DAMPING * (fine_e[i] + MID_WEIGHT * joined[fine_map[i]])

    for turn in range(3):

        @pl.when(has_low)
        def _():
            wait_for(halo_out.at[turn], halo_send.at[turn, 0])

        @pl.when(has_high)
        def _():
            wait_for(halo_out.at[turn], halo_send.at[turn, 1])

    wait_for(final.at[pl.ds(0, 3)], x_send)

    @pl.when(imports | (centre & (core == 1)))
    def _():
        wait_for(inverse_hbm, inv_send)

    @pl.when(jnp.logical_not(centre))
    def _():
        wait_for(raw_out, raw_send)

    @pl.when(centre)
    def _():
        wait_for(raw_out.at[pl.ds(0, 7)], raw_send)
        wait_for(res_in.at[pl.ds(0, 7)], res_send)
        wait_for(corr_out.at[pl.ds(0, 7)], corr_send)
        wait_for(raw_in.at[pl.ds(0, 14)], z_send)


def shards(
    right_side,
    fine_blocks,
    fine_cols,
    fine_edges,
    mid_blocks,
    mid_cols,
    mid_edges,
    fine_map,
    mid_map,
    coarse_inverse,
):
    smem = pl.BlockSpec(memory_space=pltpu.SMEM)
    anywhere = pl.BlockSpec(memory_space=pl.ANY)
    vmem = pltpu.VMEM
    dma = pltpu.SemaphoreType.DMA
    return pl.pallas_call(
        kernel,
        out_shape=jax.ShapeDtypeStruct(right_side.shape, F32),
        in_specs=[smem] * 6 + [anywhere] * 4,
        out_specs=pl.BlockSpec(memory_space=vmem),
        scratch_shapes=[
            vmem((4, 16, 128), F32),
            vmem((4, 8, 128, 128), F32),
            vmem((2, 8, 128, 128), F32),
            vmem((4, 256, 1024), BF16),
            vmem((2, 256, 1024), BF16),
            vmem((4, 16, 128), F32),
            vmem((4, 16, 128), F32),
            vmem((2, 16, 128), F32),
            vmem((2, 16, 128), F32),
            vmem((2, 16, 128), F32),
            vmem((8, 32, 128), BF16),
            vmem((4, 32, 128), BF16),
            vmem((3, 3, 16, 128), F32),
            vmem((3, 2, 3, 16, 128), F32),
            vmem((8, 8, 128), F32),
            vmem((32, 8, 128), F32),
            vmem((16, 128), F32),
            vmem((8, 16, 128), F32),
            vmem((2, 64, 1024), F32),
            vmem((256, 1024), BF16),
            vmem((8, 2, 128), F32),
            vmem((8, 2, 128), F32),
            vmem((4, 2, 8, 2, 128), F32),
            vmem((16, 128), F32),
            vmem((2, 16, 128), F32),
            dma((7,)),
            dma((3, 2)),
            dma((3, 2)),
            dma,
            dma,
            dma,
            dma,
            dma,
            dma,
            dma,
            dma,
            dma,
            dma,
            dma,
            dma,
        ],
        compiler_params=pltpu.CompilerParams(
            collective_id=0, has_side_effects=True, vmem_limit_bytes=40 * 1024 * 1024
        ),
    )(
        fine_cols,
        fine_edges,
        mid_cols,
        mid_edges,
        fine_map,
        mid_map,
        right_side,
        fine_blocks,
        mid_blocks,
        coarse_inverse,
    )


def solution(mesh):
    in_specs = (
        P("dom", "level", None),
        P("dom", None, None, None),
        P("dom", None),
        P("dom"),
        P("dom", None, None, None),
        P("dom", None),
        P("dom"),
        P("dom"),
        P("dom"),
        P("level", None),
    )
    out_specs = P("dom", "level", None)
    return jax.shard_map(shards, mesh=mesh, in_specs=in_specs, out_specs=out_specs, check_vma=False)
```

```python
import jax
import jax.numpy as jnp
from jax import lax
from jax.experimental import pallas as pl
from jax.experimental.pallas import tpu as pltpu
from jax.sharding import PartitionSpec as P

CAGG = 8
DEG = 4
CENTRE = 1.0
HALF_WIDTH = 0.7
DAMPING = 0.7
MID_WEIGHT = 0.5**0.5
COARSE_WEIGHT = CAGG**-0.5

F32 = jnp.float32
BF16 = jnp.bfloat16


def sweep_constants():
    ratio = CENTRE / HALF_WIDTH
    rho_prev = 1.0 / ratio
    constants = []
    for _ in range(DEG - 1):
        rho_next = 1.0 / (2.0 * ratio - rho_prev)
        constants.append((rho_next * rho_prev, 2.0 * rho_next / HALF_WIDTH))
        rho_prev = rho_next
    return constants


def split(value):
    high = value.astype(BF16)
    low = (value - high.astype(F32)).astype(BF16)
    return high, low


def product(left, right):
    full = lax.dot_general(left, right, (((1,), (1,)), ((), ())), preferred_element_type=F32)
    return full[:16, :128] + (full[:16, 128:] + full[16:, :128])


def wait_for(ref, sem):
    pltpu.make_async_copy(ref, ref, sem).wait()


def kernel(
    fine_cols_hbm,
    fine_edges_hbm,
    mid_cols_hbm,
    mid_edges_hbm,
    fine_map_hbm,
    mid_map_hbm,
    source_hbm,
    fine_hbm,
    mid_hbm,
    inverse_hbm,
    out,
    fine_cols,
    fine_edges,
    mid_cols,
    mid_edges,
    fine_map,
    mid_map,
    source,
    fine_raw,
    mid_raw,
    fine_w,
    mid_w,
    fine_e,
    fine_d,
    mid_g,
    mid_e,
    mid_d,
    fine_x,
    mid_x,
    halo_out,
    halo_in,
    raw_out,
    raw_in,
    res_out,
    res_in,
    inv_in,
    inv_w,
    corr_out,
    corr_in,
    final,
    picked,
    joined,
    load_sem,
    halo_send,
    halo_recv,
    raw_send,
    raw_recv,
    inv_send,
    inv_recv,
    res_send,
    res_recv,
    corr_send,
    corr_recv,
    z_send,
    z_recv,
    x_send,
    x_recv,
):
    level = lax.axis_index("level")
    dom = lax.axis_index("dom")
    half = level // 8
    mine = level % 8
    y_pos = mine // 2
    core = level % 2
    z_pos = dom // 4
    x_pos = dom % 4
    centre = (z_pos == 3) | (z_pos == 4)
    centre_i = jnp.where(centre, 1, 0)
    z_two = jnp.where(z_pos == 4, 1, 0)
    has_low = dom > 0
    has_high = dom < 31
    import_z = jnp.where(z_pos == 7, 3, 4)
    imports = (z_pos == 0) | (z_pos == 7)

    def remote(src, dst, send, recv, to_level, to_dom):
        return pltpu.make_async_remote_copy(
            src_ref=src,
            dst_ref=dst,
            send_sem=send,
            recv_sem=recv,
            device_id=(to_level, to_dom),
            device_id_type=pl.DeviceIdType.MESH,
        )

    load_small = [
        pltpu.make_async_copy(src, dst, load_sem.at[7 + n])
        for n, (src, dst) in enumerate(
            [
                (fine_map_hbm, fine_map),
                (mid_map_hbm, mid_map),
                (fine_edges_hbm, fine_edges),
                (mid_edges_hbm, mid_edges),
                (fine_cols_hbm, fine_cols),
                (mid_cols_hbm, mid_cols),
            ]
        )
    ]
    load_source = pltpu.make_async_copy(source_hbm, source, load_sem.at[0])
    load_source.start()
    for load in load_small:
        load.start()
    load_fine = [
        pltpu.make_async_copy(fine_hbm.at[r], fine_raw.at[r], load_sem.at[1 + r]) for r in range(4)
    ]
    load_mid = [
        pltpu.make_async_copy(mid_hbm.at[r], mid_raw.at[r], load_sem.at[5 + r]) for r in range(2)
    ]
    for load in load_fine + load_mid:
        load.start()

    barrier = pltpu.get_barrier_semaphore()

    def greet(to_level, to_dom):
        pl.semaphore_signal(
            barrier, inc=1, device_id=(to_level, to_dom), device_id_type=pl.DeviceIdType.MESH
        )

    @pl.when(has_low)
    def _():
        greet(level, dom - 1)

    @pl.when(has_high)
    def _():
        greet(level, dom + 1)

    for other_z in (3, 4):

        @pl.when(z_pos != other_z)
        def _():
            greet(level, other_z * 4 + x_pos)

    for step in range(1, 4):
        greet(level, z_pos * 4 + (x_pos + step) % 4)

    @pl.when(centre)
    def _():
        @pl.loop(1, 32)
        def _(step):
            greet(level, (dom + step) % 32)

        @pl.loop(1, 8)
        def _(step):
            greet(half * 8 + (mine + step) % 8, dom)

        @pl.when(core == 0)
        def _():
            greet(level + 1, dom)

        @pl.when(core == 1)
        def _():
            from_dom = jnp.where(z_pos == 3, 7, 0) * 4 + x_pos
            greet((1 - half) * 8 + y_pos * 2, from_dom)
            greet((1 - half) * 8 + y_pos * 2 + 1, from_dom)

    for load in load_small:
        load.wait()
    load_source.wait()
    lanes = lax.broadcasted_iota(jnp.int32, (1, 128), 1)
    for j in range(2):
        total = None
        for i in range(4):
            term = jnp.where(fine_map[i] == j, source[i], 0.0)
            total = term if total is None else total + term
        mid_g[j] = MID_WEIGHT * total
    raw_out[:, 6:8, :] = jnp.zeros((8, 2, 128), F32)
    for j in range(2):
        row = jnp.where((lanes < 16) & (lanes % 8 == mid_map[j]), 1.0, 0.0)
        for n in range(8):
            first = 4 * (n % 4) + 2 * (n // 4)
            raw_out[n, 2 * j : 2 * j + 2, :] = mid_g[j, first : first + 2, :]
            raw_out[n, 4 + j : 5 + j, :] = row

    def fill_halo(turn, fine_ref, mid_ref):
        halo_out[turn, 0] = fine_ref[fine_edges[0]]
        halo_out[turn, 1] = fine_ref[fine_edges[1]]
        halo_out[turn, 2] = mid_ref[mid_edges[0]]

    fill_halo(0, source, mid_g)

    @pl.when(dom == 0)
    def _():
        for turn in range(3):
            halo_in[turn, 0] = jnp.zeros((3, 16, 128), F32)

    @pl.when(dom == 31)
    def _():
        for turn in range(3):
            halo_in[turn, 1] = jnp.zeros((3, 16, 128), F32)

    sides = jnp.where(has_low, 1, 0) + jnp.where(has_high, 1, 0)
    waits = sides + 8 - centre_i + 3 + 14 * centre_i
    waits = waits + jnp.where(imports, 1, 0) + centre_i * core
    pl.semaphore_wait(barrier, waits)

    def halo_low(turn):
        return remote(
            halo_out.at[turn],
            halo_in.at[turn, 1],
            halo_send.at[turn, 0],
            halo_recv.at[turn, 1],
            level,
            dom - 1,
        )

    def halo_high(turn):
        return remote(
            halo_out.at[turn],
            halo_in.at[turn, 0],
            halo_send.at[turn, 1],
            halo_recv.at[turn, 0],
            level,
            dom + 1,
        )

    def start_halo(turn):
        @pl.when(has_low)
        def _():
            halo_low(turn).start()

        @pl.when(has_high)
        def _():
            halo_high(turn).start()

    def wait_halo(turn):
        @pl.when(has_low)
        def _():
            wait_for(halo_in.at[turn, 0], halo_recv.at[turn, 0])

        @pl.when(has_high)
        def _():
            wait_for(halo_in.at[turn, 1], halo_recv.at[turn, 1])

    start_halo(0)

    @pl.loop(0, 8)
    def _(n):
        to_dom = (3 + n // 4) * 4 + n % 4

        @pl.when(to_dom != dom)
        def _():
            remote(raw_out.at[n], raw_in.at[dom], raw_send, raw_recv, level, to_dom).start()

        @pl.when(to_dom == dom)
        def _():
            pltpu.make_async_copy(raw_out.at[n], raw_in.at[dom], raw_recv).start()

    @pl.when(centre & (core == 0))
    def _():
        pltpu.make_async_copy(inverse_hbm, inv_in.at[0], inv_recv).start()

    @pl.when(centre & (core == 1))
    def _():
        remote(inverse_hbm, inv_in.at[1], inv_send, inv_recv, level - 1, dom).start()

    @pl.when(imports)
    def _():
        remote(
            inverse_hbm,
            inv_in.at[core],
            inv_send,
            inv_recv,
            (1 - half) * 8 + y_pos * 2 + 1,
            import_z * 4 + x_pos,
        ).start()

    for r in range(4):
        load_fine[r].wait()
        for k in range(8):
            high, low = split(fine_raw[r, k])
            fine_w[r, 0:128, k * 128 : k * 128 + 128] = high
            fine_w[r, 128:256, k * 128 : k * 128 + 128] = low
    for r in range(2):
        load_mid[r].wait()
        for k in range(8):
            high, low = split(mid_raw[r, k])
            mid_w[r, 0:128, k * 128 : k * 128 + 128] = high
            mid_w[r, 128:256, k * 128 : k * 128 + 128] = low

    def put(ref, slot, value):
        high, low = split(value)
        ref[slot, 0:16, :] = high
        ref[slot, 16:32, :] = low

    constants = sweep_constants()

    def sweep(turn):
        keep, push = constants[turn]
        old_fine = source if turn == 0 else fine_e
        old_mid = mid_g if turn == 0 else mid_e
        old_fine_d = source if turn == 0 else fine_d
        old_mid_d = mid_g if turn == 0 else mid_d
        for r in range(4):
            put(fine_x, r, old_fine[r])
        for r in range(2):
            put(mid_x, r, old_mid[r])
        wait_halo(turn)
        for side in range(2):
            for row in range(2):
                put(fine_x, 4 + 2 * side + row, halo_in[turn, side, row])
            put(mid_x, 2 + side, halo_in[turn, side, 2])
        for r in range(4):
            left = jnp.concatenate([fine_x[fine_cols[r, k]] for k in range(8)], axis=1)
            applied = old_fine[r] + product(left, fine_w[r])
            step = keep * old_fine_d[r] + push * (source[r] - applied)
            fine_d[r] = step
            fine_e[r] = old_fine[r] + step
        for r in range(2):
            left = jnp.concatenate([mid_x[mid_cols[r, k]] for k in range(8)], axis=1)
            applied = old_mid[r] + product(left, mid_w[r])
            step = keep * old_mid_d[r] + push * (mid_g[r] - applied)
            mid_d[r] = step
            mid_e[r] = old_mid[r] + step
        if turn < 2:
            fill_halo(turn + 1, fine_e, mid_e)
            start_halo(turn + 1)

    sweep(0)

    @pl.when(centre)
    def _():
        wait_for(raw_in, raw_recv)
        rows = lax.broadcasted_iota(jnp.int32, (32, 8, 128), 1)
        cols = lax.broadcasted_iota(jnp.int32, (32, 8, 128), 2)
        value = raw_in[...]
        first = jnp.broadcast_to(value[:, 4:5, :], (32, 8, 128))
        second = jnp.broadcast_to(value[:, 5:6, :], (32, 8, 128))
        picks = jnp.where(rows < 2, first, second)
        wanted = (rows < 4) & (cols // 8 == rows % 2)
        picks = jnp.where(wanted, picks, 0.0).reshape(256, 128).astype(BF16)
        high, low = split(value.reshape(256, 128))
        both = jnp.concatenate([high, low], axis=1)
        full = lax.dot_general(picks, both, (((0,), (0,)), ((), ())), preferred_element_type=F32)
        total = full[:16, :128] + full[:16, 128:]
        res_out[...] = total

        @pl.loop(0, 8)
        def _(peer):
            @pl.when(peer != mine)
            def _():
                remote(res_out, res_in.at[mine], res_send, res_recv, half * 8 + peer, dom).start()

            @pl.when(peer == mine)
            def _():
                pltpu.make_async_copy(res_out, res_in.at[mine], res_recv).start()

    sweep(1)

    @pl.when(centre)
    def _():
        wait_for(inv_in, inv_recv)
        for h in range(2):
            high, low = split(inv_in[h])
            inv_w[64 * h : 64 * h + 64, :] = high
            inv_w[128 + 64 * h : 192 + 64 * h, :] = low
        wait_for(res_in, res_recv)
        parts = []
        for c in range(8):
            block = jnp.concatenate([res_in[:, c, :], res_in[:, 8 + c, :]], axis=0)
            high, low = split(block)
            parts.append(jnp.concatenate([high, low], axis=0))
        left = jnp.concatenate(parts, axis=1)
        corr = product(left, inv_w[...])
        for peer in range(8):
            corr_out[peer, 0:1, :] = corr[peer : peer + 1, :]
            corr_out[peer, 1:2, :] = corr[8 + peer : 9 + peer, :]
        row = jnp.where(core == 0, half, 1 - half) * 4 + y_pos

        @pl.loop(0, 8)
        def _(peer):
            @pl.when(peer != mine)
            def _():
                remote(
                    corr_out.at[peer], corr_in.at[row], corr_send, corr_recv, half * 8 + peer, dom
                ).start()

            @pl.when(peer == mine)
            def _():
                pltpu.make_async_copy(corr_out.at[peer], corr_in.at[row], corr_recv).start()

    sweep(2)

    @pl.when(centre)
    def _():
        wait_for(corr_in, corr_recv)

        @pl.loop(0, 8)
        def _(other_z):
            @pl.when(other_z != z_pos)
            def _():
                remote(
                    corr_in,
                    final.at[x_pos, z_two],
                    z_send,
                    z_recv,
                    level,
                    other_z * 4 + x_pos,
                ).start()

            @pl.when(other_z == z_pos)
            def _():
                pltpu.make_async_copy(corr_in, final.at[x_pos, z_two], z_recv).start()

    wait_for(final.at[0], z_recv)

    for step in range(1, 4):
        remote(
            final.at[x_pos],
            final.at[x_pos],
            x_send,
            x_recv,
            level,
            z_pos * 4 + (x_pos + step) % 4,
        ).start()
    wait_for(final.at[pl.ds(0, 3)], x_recv)

    for j in range(2):
        for n in range(8):
            first = 4 * (n // 2) + 2 * (n % 2)
            picked[first : first + 2, :] = final[n // 2, n % 2, mid_map[j]]
        joined[j] = mid_e[j] + (COARSE_WEIGHT * COARSE_WEIGHT) * picked[...]
    for i in range(4):
        out[i] = DAMPING * (fine_e[i] + MID_WEIGHT * joined[fine_map[i]])

    for turn in range(3):

        @pl.when(has_low)
        def _():
            wait_for(halo_out.at[turn], halo_send.at[turn, 0])

        @pl.when(has_high)
        def _():
            wait_for(halo_out.at[turn], halo_send.at[turn, 1])

    wait_for(final.at[pl.ds(0, 3)], x_send)

    @pl.when(imports | (centre & (core == 1)))
    def _():
        wait_for(inverse_hbm, inv_send)

    @pl.when(jnp.logical_not(centre))
    def _():
        wait_for(raw_out, raw_send)

    @pl.when(centre)
    def _():
        wait_for(raw_out.at[pl.ds(0, 7)], raw_send)
        wait_for(res_in.at[pl.ds(0, 7)], res_send)
        wait_for(corr_out.at[pl.ds(0, 7)], corr_send)
        wait_for(raw_in.at[pl.ds(0, 14)], z_send)


def shards(
    right_side,
    fine_blocks,
    fine_cols,
    fine_edges,
    mid_blocks,
    mid_cols,
    mid_edges,
    fine_map,
    mid_map,
    coarse_inverse,
):
    hbm = pl.BlockSpec(memory_space=pltpu.HBM)
    smem = pltpu.SMEM
    vmem = pltpu.VMEM
    dma = pltpu.SemaphoreType.DMA
    return pl.pallas_call(
        kernel,
        out_shape=jax.ShapeDtypeStruct(right_side.shape, F32),
        in_specs=[hbm] * 10,
        out_specs=pl.BlockSpec(memory_space=vmem),
        scratch_shapes=[
            smem((4, 8), jnp.int32),
            smem((2,), jnp.int32),
            smem((2, 8), jnp.int32),
            smem((1,), jnp.int32),
            smem((4,), jnp.int32),
            smem((2,), jnp.int32),
            vmem((4, 16, 128), F32),
            vmem((4, 8, 128, 128), F32),
            vmem((2, 8, 128, 128), F32),
            vmem((4, 256, 1024), BF16),
            vmem((2, 256, 1024), BF16),
            vmem((4, 16, 128), F32),
            vmem((4, 16, 128), F32),
            vmem((2, 16, 128), F32),
            vmem((2, 16, 128), F32),
            vmem((2, 16, 128), F32),
            vmem((8, 32, 128), BF16),
            vmem((4, 32, 128), BF16),
            vmem((3, 3, 16, 128), F32),
            vmem((3, 2, 3, 16, 128), F32),
            vmem((8, 8, 128), F32),
            vmem((32, 8, 128), F32),
            vmem((16, 128), F32),
            vmem((8, 16, 128), F32),
            vmem((2, 64, 1024), F32),
            vmem((256, 1024), BF16),
            vmem((8, 2, 128), F32),
            vmem((8, 2, 128), F32),
            vmem((4, 2, 8, 2, 128), F32),
            vmem((16, 128), F32),
            vmem((2, 16, 128), F32),
            dma((13,)),
            dma((3, 2)),
            dma((3, 2)),
            dma,
            dma,
            dma,
            dma,
            dma,
            dma,
            dma,
            dma,
            dma,
            dma,
            dma,
            dma,
        ],
        compiler_params=pltpu.CompilerParams(
            collective_id=0, has_side_effects=True, vmem_limit_bytes=67043328
        ),
    )(
        fine_cols,
        fine_edges,
        mid_cols,
        mid_edges,
        fine_map,
        mid_map,
        right_side,
        fine_blocks,
        mid_blocks,
        coarse_inverse,
    )


def solution(mesh):
    in_specs = (
        P("dom", "level", None),
        P("dom", None, None, None),
        P("dom", None),
        P("dom"),
        P("dom", None, None, None),
        P("dom", None),
        P("dom"),
        P("dom"),
        P("dom"),
        P("level", None),
    )
    out_specs = P("dom", "level", None)
    return jax.shard_map(shards, mesh=mesh, in_specs=in_specs, out_specs=out_specs, check_vma=False)
```

```python
import jax
import jax.numpy as jnp
from jax import lax
from jax.experimental import pallas as pl
from jax.experimental.pallas import tpu as pltpu
from jax.sharding import PartitionSpec as P

CAGG = 8
DEG = 4
CENTRE = 1.0
HALF_WIDTH = 0.7
DAMPING = 0.7
MID_WEIGHT = 0.5**0.5
COARSE_WEIGHT = CAGG**-0.5

F32 = jnp.float32
BF16 = jnp.bfloat16


def sweep_constants():
    ratio = CENTRE / HALF_WIDTH
    rho_prev = 1.0 / ratio
    constants = []
    for _ in range(DEG - 1):
        rho_next = 1.0 / (2.0 * ratio - rho_prev)
        constants.append((rho_next * rho_prev, 2.0 * rho_next / HALF_WIDTH))
        rho_prev = rho_next
    return constants


def split(value):
    high = value.astype(BF16)
    low = (value - high.astype(F32)).astype(BF16)
    return high, low


def product(left, right):
    full = lax.dot_general(left, right, (((1,), (1,)), ((), ())), preferred_element_type=F32)
    return full[:16, :128] + (full[:16, 128:] + full[16:, :128])


def wait_for(ref, sem):
    pltpu.make_async_copy(ref, ref, sem).wait()


def kernel(
    fine_cols_hbm,
    fine_edges_hbm,
    mid_cols_hbm,
    mid_edges_hbm,
    fine_map_hbm,
    mid_map_hbm,
    source_hbm,
    fine_hbm,
    mid_hbm,
    inverse_hbm,
    out,
    fine_cols,
    fine_edges,
    mid_cols,
    mid_edges,
    fine_map,
    mid_map,
    source,
    fine_raw,
    mid_raw,
    fine_w,
    mid_w,
    fine_e,
    fine_d,
    mid_g,
    mid_e,
    mid_d,
    fine_x,
    mid_x,
    halo_out,
    halo_in,
    raw_out,
    raw_in,
    res_out,
    res_in,
    inv_in,
    inv_w,
    corr_out,
    spare,
    final,
    picked,
    joined,
    load_sem,
    halo_send,
    halo_recv,
    raw_send,
    raw_recv,
    inv_send,
    inv_recv,
    res_send,
    res_recv,
    z_send,
    z_recv,
    x_send,
    x_recv,
):
    level = lax.axis_index("level")
    dom = lax.axis_index("dom")
    half = level // 8
    mine = level % 8
    y_pos = mine // 2
    core = level % 2
    z_pos = dom // 4
    x_pos = dom % 4
    centre = (z_pos == 3) | (z_pos == 4)
    centre_i = jnp.where(centre, 1, 0)
    z_two = jnp.where(z_pos == 4, 1, 0)
    has_low = dom > 0
    has_high = dom < 31
    import_z = jnp.where(z_pos == 7, 3, 4)
    imports = (z_pos == 0) | (z_pos == 7)

    def remote(src, dst, send, recv, to_level, to_dom):
        return pltpu.make_async_remote_copy(
            src_ref=src,
            dst_ref=dst,
            send_sem=send,
            recv_sem=recv,
            device_id=(to_level, to_dom),
            device_id_type=pl.DeviceIdType.MESH,
        )

    load_small = [
        pltpu.make_async_copy(src, dst, load_sem.at[7 + n])
        for n, (src, dst) in enumerate(
            [
                (fine_map_hbm, fine_map),
                (mid_map_hbm, mid_map),
                (fine_edges_hbm, fine_edges),
                (mid_edges_hbm, mid_edges),
                (fine_cols_hbm, fine_cols),
                (mid_cols_hbm, mid_cols),
            ]
        )
    ]
    load_source = pltpu.make_async_copy(source_hbm, source, load_sem.at[0])
    load_source.start()
    for load in load_small:
        load.start()
    load_fine = [
        pltpu.make_async_copy(fine_hbm.at[r], fine_raw.at[r], load_sem.at[1 + r]) for r in range(4)
    ]
    load_mid = [
        pltpu.make_async_copy(mid_hbm.at[r], mid_raw.at[r], load_sem.at[5 + r]) for r in range(2)
    ]
    for load in load_fine + load_mid:
        load.start()

    barrier = pltpu.get_barrier_semaphore()

    def greet(to_level, to_dom):
        pl.semaphore_signal(
            barrier, inc=1, device_id=(to_level, to_dom), device_id_type=pl.DeviceIdType.MESH
        )

    @pl.when(has_low)
    def _():
        greet(level, dom - 1)

    @pl.when(has_high)
    def _():
        greet(level, dom + 1)

    for other_z in (3, 4):
        for peer in range(8):

            @pl.when((z_pos != other_z) | (mine != peer))
            def _():
                greet(half * 8 + peer, other_z * 4 + x_pos)

    for step in range(1, 4):
        greet(level, z_pos * 4 + (x_pos + step) % 4)

    @pl.when(centre)
    def _():
        @pl.loop(1, 32)
        def _(step):
            greet(level, (dom + step) % 32)

        @pl.when(core == 0)
        def _():
            greet(level + 1, dom)

        @pl.when(core == 1)
        def _():
            from_dom = jnp.where(z_pos == 3, 7, 0) * 4 + x_pos
            greet((1 - half) * 8 + y_pos * 2, from_dom)
            greet((1 - half) * 8 + y_pos * 2 + 1, from_dom)

    for load in load_small:
        load.wait()
    load_source.wait()
    lanes = lax.broadcasted_iota(jnp.int32, (1, 128), 1)
    for j in range(2):
        total = None
        for i in range(4):
            term = jnp.where(fine_map[i] == j, source[i], 0.0)
            total = term if total is None else total + term
        mid_g[j] = MID_WEIGHT * total
    wanted = jnp.where(lanes < 64, mid_map[0], mid_map[1])
    row = jnp.where((lanes % 64 < 16) & (lanes % 8 == wanted), 1.0, 0.0)
    for n in range(8):
        first = 4 * (n % 4) + 2 * (n // 4)
        for j in range(2):
            raw_out[n, 2 * j : 2 * j + 2, :] = mid_g[j, first : first + 2, :]
        raw_out[n, 4:5, :] = row

    def fill_halo(turn, fine_ref, mid_ref):
        halo_out[turn, 0] = fine_ref[fine_edges[0]]
        halo_out[turn, 1] = fine_ref[fine_edges[1]]
        halo_out[turn, 2] = mid_ref[mid_edges[0]]

    fill_halo(0, source, mid_g)

    @pl.when(dom == 0)
    def _():
        for turn in range(3):
            halo_in[turn, 0] = jnp.zeros((3, 16, 128), F32)

    @pl.when(dom == 31)
    def _():
        for turn in range(3):
            halo_in[turn, 1] = jnp.zeros((3, 16, 128), F32)

    @pl.when(centre)
    def _():
        raw_in[:, 5:8, :] = jnp.zeros((32, 3, 128), F32)

    sides = jnp.where(has_low, 1, 0) + jnp.where(has_high, 1, 0)
    waits = sides + 8 - centre_i + 3 + 63 * centre_i
    waits = waits + jnp.where(imports, 1, 0) + centre_i * core
    pl.semaphore_wait(barrier, waits)

    def halo_low(turn):
        return remote(
            halo_out.at[turn],
            halo_in.at[turn, 1],
            halo_send.at[turn, 0],
            halo_recv.at[turn, 1],
            level,
            dom - 1,
        )

    def halo_high(turn):
        return remote(
            halo_out.at[turn],
            halo_in.at[turn, 0],
            halo_send.at[turn, 1],
            halo_recv.at[turn, 0],
            level,
            dom + 1,
        )

    def start_halo(turn):
        @pl.when(has_low)
        def _():
            halo_low(turn).start()

        @pl.when(has_high)
        def _():
            halo_high(turn).start()

    def wait_halo(turn):
        @pl.when(has_low)
        def _():
            wait_for(halo_in.at[turn, 0], halo_recv.at[turn, 0])

        @pl.when(has_high)
        def _():
            wait_for(halo_in.at[turn, 1], halo_recv.at[turn, 1])

    raw_slot = raw_in.at[dom, pl.ds(0, 5)]
    for n in range(8):
        to_dom = (3 + n // 4) * 4 + n % 4

        @pl.when(to_dom != dom)
        def _():
            remote(raw_out.at[n], raw_slot, raw_send, raw_recv, level, to_dom).start()

        @pl.when(to_dom == dom)
        def _():
            pltpu.make_async_copy(raw_out.at[n], raw_slot, raw_recv).start()

    start_halo(0)

    @pl.when(centre & (core == 0))
    def _():
        pltpu.make_async_copy(inverse_hbm, inv_in.at[0], inv_recv).start()

    @pl.when(centre & (core == 1))
    def _():
        remote(inverse_hbm, inv_in.at[1], inv_send, inv_recv, level - 1, dom).start()

    @pl.when(imports)
    def _():
        remote(
            inverse_hbm,
            inv_in.at[core],
            inv_send,
            inv_recv,
            (1 - half) * 8 + y_pos * 2 + 1,
            import_z * 4 + x_pos,
        ).start()

    for r in range(4):
        load_fine[r].wait()
        for k in range(8):
            high, low = split(fine_raw[r, k])
            fine_w[r, 0:128, k * 128 : k * 128 + 128] = high
            fine_w[r, 128:256, k * 128 : k * 128 + 128] = low
    for r in range(2):
        load_mid[r].wait()
        for k in range(8):
            high, low = split(mid_raw[r, k])
            mid_w[r, 0:128, k * 128 : k * 128 + 128] = high
            mid_w[r, 128:256, k * 128 : k * 128 + 128] = low

    def put(ref, slot, value):
        high, low = split(value)
        ref[slot, 0:16, :] = high
        ref[slot, 16:32, :] = low

    constants = sweep_constants()

    def sweep(turn):
        keep, push = constants[turn]
        old_fine = source if turn == 0 else fine_e
        old_mid = mid_g if turn == 0 else mid_e
        old_fine_d = source if turn == 0 else fine_d
        old_mid_d = mid_g if turn == 0 else mid_d
        for r in range(4):
            put(fine_x, r, old_fine[r])
        for r in range(2):
            put(mid_x, r, old_mid[r])
        wait_halo(turn)
        for side in range(2):
            for row in range(2):
                put(fine_x, 4 + 2 * side + row, halo_in[turn, side, row])
            put(mid_x, 2 + side, halo_in[turn, side, 2])
        for r in range(4):
            left = jnp.concatenate([fine_x[fine_cols[r, k]] for k in range(8)], axis=1)
            applied = old_fine[r] + product(left, fine_w[r])
            step = keep * old_fine_d[r] + push * (source[r] - applied)
            fine_d[r] = step
            fine_e[r] = old_fine[r] + step
        for r in range(2):
            left = jnp.concatenate([mid_x[mid_cols[r, k]] for k in range(8)], axis=1)
            applied = old_mid[r] + product(left, mid_w[r])
            step = keep * old_mid_d[r] + push * (mid_g[r] - applied)
            mid_d[r] = step
            mid_e[r] = old_mid[r] + step
        if turn < 2:
            fill_halo(turn + 1, fine_e, mid_e)
            start_halo(turn + 1)


    @pl.when(centre)
    def _():
        wait_for(raw_in.at[:, pl.ds(0, 5)], raw_recv)
        rows = lax.broadcasted_iota(jnp.int32, (32, 8, 128), 1)
        cols = lax.broadcasted_iota(jnp.int32, (32, 8, 128), 2)
        value = raw_in[...]
        first = jnp.broadcast_to(value[:, 4:5, :], (32, 8, 128))
        second = pltpu.roll(first, 64, 2)
        picks = jnp.where(rows < 2, first, second)
        wanted = (rows < 4) & (cols // 8 == rows % 2)
        picks = jnp.where(wanted, picks, 0.0).reshape(256, 128).astype(BF16)
        high, low = split(value.reshape(256, 128))
        both = jnp.concatenate([high, low], axis=1)
        full = lax.dot_general(picks, both, (((0,), (0,)), ((), ())), preferred_element_type=F32)
        total = full[:16, :128] + full[:16, 128:]
        res_out[...] = total

        @pl.loop(0, 8)
        def _(peer):
            @pl.when(peer != mine)
            def _():
                remote(res_out, res_in.at[mine], res_send, res_recv, half * 8 + peer, dom).start()

            @pl.when(peer == mine)
            def _():
                pltpu.make_async_copy(res_out, res_in.at[mine], res_recv).start()

    sweep(0)

    @pl.when(centre)
    def _():
        wait_for(inv_in, inv_recv)
        for h in range(2):
            high, low = split(inv_in[h])
            inv_w[64 * h : 64 * h + 64, :] = high
            inv_w[128 + 64 * h : 192 + 64 * h, :] = low
        wait_for(res_in, res_recv)
        parts = []
        for c in range(8):
            block = jnp.concatenate([res_in[:, c, :], res_in[:, 8 + c, :]], axis=0)
            high, low = split(block)
            parts.append(jnp.concatenate([high, low], axis=0))
        left = jnp.concatenate(parts, axis=1)
        corr = product(left, inv_w[...])
        for peer in range(8):
            corr_out[peer, 0:1, :] = corr[peer : peer + 1, :]
            corr_out[peer, 1:2, :] = corr[8 + peer : 9 + peer, :]
        row = jnp.where(core == 0, half, 1 - half) * 4 + y_pos

        slot = final.at[x_pos, z_two, row]

        def result_to(peer, other_z):
            return remote(
                corr_out.at[peer],
                slot,
                z_send,
                z_recv.at[z_two],
                half * 8 + peer,
                other_z * 4 + x_pos,
            )

        @pl.loop(0, 7)
        def _(step):
            other_z = (z_pos + 4 + step + jnp.where(step > 3, 1, 0)) % 8
            for peer in range(8):
                result_to(peer, other_z).start()

        for peer in range(8):

            @pl.when(peer != mine)
            def _():
                result_to(peer, z_pos).start()

            @pl.when(peer == mine)
            def _():
                pltpu.make_async_copy(corr_out.at[peer], slot, z_recv.at[z_two]).start()

    sweep(1)
    sweep(2)
    for which in range(2):
        wait_for(final.at[0, which], z_recv.at[which])
        for step in range(1, 4):
            remote(
                final.at[x_pos, which],
                final.at[x_pos, which],
                x_send,
                x_recv,
                level,
                z_pos * 4 + (x_pos + step) % 4,
            ).start()
    wait_for(final.at[pl.ds(0, 3)], x_recv)

    for j in range(2):
        for n in range(8):
            first = 4 * (n // 2) + 2 * (n % 2)
            picked[first : first + 2, :] = final[n // 2, n % 2, mid_map[j]]
        joined[j] = mid_e[j] + (COARSE_WEIGHT * COARSE_WEIGHT) * picked[...]
    for i in range(4):
        out[i] = DAMPING * (fine_e[i] + MID_WEIGHT * joined[fine_map[i]])

    for turn in range(3):

        @pl.when(has_low)
        def _():
            wait_for(halo_out.at[turn], halo_send.at[turn, 0])

        @pl.when(has_high)
        def _():
            wait_for(halo_out.at[turn], halo_send.at[turn, 1])

    wait_for(final.at[pl.ds(0, 3)], x_send)

    @pl.when(imports | (centre & (core == 1)))
    def _():
        wait_for(inverse_hbm, inv_send)

    @pl.when(jnp.logical_not(centre))
    def _():
        wait_for(raw_out, raw_send)

    @pl.when(centre)
    def _():
        wait_for(raw_out.at[pl.ds(0, 7)], raw_send)
        wait_for(res_in.at[pl.ds(0, 7)], res_send)
        wait_for(spare, z_send)


def shards(
    right_side,
    fine_blocks,
    fine_cols,
    fine_edges,
    mid_blocks,
    mid_cols,
    mid_edges,
    fine_map,
    mid_map,
    coarse_inverse,
):
    hbm = pl.BlockSpec(memory_space=pltpu.HBM)
    smem = pltpu.SMEM
    vmem = pltpu.VMEM
    dma = pltpu.SemaphoreType.DMA
    return pl.pallas_call(
        kernel,
        out_shape=jax.ShapeDtypeStruct(right_side.shape, F32),
        in_specs=[hbm] * 10,
        out_specs=pl.BlockSpec(memory_space=vmem),
        scratch_shapes=[
            smem((4, 8), jnp.int32),
            smem((2,), jnp.int32),
            smem((2, 8), jnp.int32),
            smem((1,), jnp.int32),
            smem((4,), jnp.int32),
            smem((2,), jnp.int32),
            vmem((4, 16, 128), F32),
            vmem((4, 8, 128, 128), F32),
            vmem((2, 8, 128, 128), F32),
            vmem((4, 256, 1024), BF16),
            vmem((2, 256, 1024), BF16),
            vmem((4, 16, 128), F32),
            vmem((4, 16, 128), F32),
            vmem((2, 16, 128), F32),
            vmem((2, 16, 128), F32),
            vmem((2, 16, 128), F32),
            vmem((8, 32, 128), BF16),
            vmem((4, 32, 128), BF16),
            vmem((3, 3, 16, 128), F32),
            vmem((3, 2, 3, 16, 128), F32),
            vmem((8, 5, 128), F32),
            vmem((32, 8, 128), F32),
            vmem((16, 128), F32),
            vmem((8, 16, 128), F32),
            vmem((2, 64, 1024), F32),
            vmem((256, 1024), BF16),
            vmem((8, 2, 128), F32),
            vmem((63, 2, 128), F32),
            vmem((4, 2, 8, 2, 128), F32),
            vmem((16, 128), F32),
            vmem((2, 16, 128), F32),
            dma((13,)),
            dma((3, 2)),
            dma((3, 2)),
            dma,
            dma,
            dma,
            dma,
            dma,
            dma,
            dma,
            dma((2,)),
            dma,
            dma,
        ],
        compiler_params=pltpu.CompilerParams(
            collective_id=0, has_side_effects=True, vmem_limit_bytes=67043328
        ),
    )(
        fine_cols,
        fine_edges,
        mid_cols,
        mid_edges,
        fine_map,
        mid_map,
        right_side,
        fine_blocks,
        mid_blocks,
        coarse_inverse,
    )


def solution(mesh):
    in_specs = (
        P("dom", "level", None),
        P("dom", None, None, None),
        P("dom", None),
        P("dom"),
        P("dom", None, None, None),
        P("dom", None),
        P("dom"),
        P("dom"),
        P("dom"),
        P("level", None),
    )
    out_specs = P("dom", "level", None)
    return jax.shard_map(shards, mesh=mesh, in_specs=in_specs, out_specs=out_specs, check_vma=False)
```

```python
import jax
import jax.numpy as jnp
from jax import lax
from jax.experimental import pallas as pl
from jax.experimental.pallas import tpu as pltpu
from jax.sharding import PartitionSpec as P

CAGG = 8
DEG = 4
CENTRE = 1.0
HALF_WIDTH = 0.7
DAMPING = 0.7
MID_WEIGHT = 0.5**0.5
COARSE_WEIGHT = CAGG**-0.5

F32 = jnp.float32
BF16 = jnp.bfloat16


def sweep_constants():
    ratio = CENTRE / HALF_WIDTH
    rho_prev = 1.0 / ratio
    constants = []
    for _ in range(DEG - 1):
        rho_next = 1.0 / (2.0 * ratio - rho_prev)
        constants.append((rho_next * rho_prev, 2.0 * rho_next / HALF_WIDTH))
        rho_prev = rho_next
    return constants


def split(value):
    high = value.astype(BF16)
    low = (value - high.astype(F32)).astype(BF16)
    return high, low


def product(left, right):
    full = lax.dot_general(left, right, (((1,), (1,)), ((), ())), preferred_element_type=F32)
    return full[:16, :128] + (full[:16, 128:] + full[16:, :128])


def wait_for(ref, sem):
    pltpu.make_async_copy(ref, ref, sem).wait()


def kernel(
    fine_cols_hbm,
    fine_edges_hbm,
    mid_cols_hbm,
    mid_edges_hbm,
    fine_map_hbm,
    mid_map_hbm,
    source_hbm,
    fine_hbm,
    mid_hbm,
    inverse_hbm,
    out,
    fine_cols,
    fine_edges,
    mid_cols,
    mid_edges,
    fine_map,
    mid_map,
    source,
    fine_raw,
    mid_raw,
    fine_w,
    mid_w,
    fine_e,
    fine_d,
    mid_g,
    mid_e,
    mid_d,
    fine_x,
    mid_x,
    halo_out,
    halo_in,
    raw_out,
    raw_in,
    res_out,
    res_in,
    inv_in,
    inv_w,
    corr_out,
    spare,
    final,
    picked,
    joined,
    partial,
    load_sem,
    halo_send,
    halo_recv,
    raw_send,
    raw_recv,
    inv_send,
    inv_recv,
    res_send,
    res_recv,
    z_send,
    z_recv,
    x_send,
    x_recv,
):
    level = lax.axis_index("level")
    dom = lax.axis_index("dom")
    half = level // 8
    mine = level % 8
    y_pos = mine // 2
    core = level % 2
    z_pos = dom // 4
    x_pos = dom % 4
    centre = (z_pos == 3) | (z_pos == 4)
    centre_i = jnp.where(centre, 1, 0)
    z_two = jnp.where(z_pos == 4, 1, 0)
    has_low = dom > 0
    has_high = dom < 31
    import_z = jnp.where(z_pos == 7, 3, 4)
    imports = (z_pos == 0) | (z_pos == 7)

    def remote(src, dst, send, recv, to_level, to_dom):
        return pltpu.make_async_remote_copy(
            src_ref=src,
            dst_ref=dst,
            send_sem=send,
            recv_sem=recv,
            device_id=(to_level, to_dom),
            device_id_type=pl.DeviceIdType.MESH,
        )

    load_small = [
        pltpu.make_async_copy(src, dst, load_sem.at[7 + n])
        for n, (src, dst) in enumerate(
            [
                (fine_map_hbm, fine_map),
                (mid_map_hbm, mid_map),
                (fine_edges_hbm, fine_edges),
                (mid_edges_hbm, mid_edges),
                (fine_cols_hbm, fine_cols),
                (mid_cols_hbm, mid_cols),
            ]
        )
    ]
    load_source = pltpu.make_async_copy(source_hbm, source, load_sem.at[0])
    for load in load_small[:2] + [load_source] + load_small[2:]:
        load.start()
    load_fine = [
        pltpu.make_async_copy(fine_hbm.at[r], fine_raw.at[r], load_sem.at[1 + r]) for r in range(4)
    ]
    load_mid = [
        pltpu.make_async_copy(mid_hbm.at[r], mid_raw.at[r], load_sem.at[5 + r]) for r in range(2)
    ]
    barrier = pltpu.get_barrier_semaphore()

    def greet(to_level, to_dom):
        pl.semaphore_signal(
            barrier, inc=1, device_id=(to_level, to_dom), device_id_type=pl.DeviceIdType.MESH
        )

    @pl.when(has_low)
    def _():
        greet(level, dom - 1)

    @pl.when(has_high)
    def _():
        greet(level, dom + 1)

    for other_z in (3, 4):
        for peer in range(8):

            @pl.when((z_pos != other_z) | (mine != peer))
            def _():
                greet(half * 8 + peer, other_z * 4 + x_pos)

    for step in range(1, 4):
        greet(level, z_pos * 4 + (x_pos + step) % 4)

    @pl.when(centre)
    def _():
        @pl.loop(1, 32)
        def _(step):
            greet(level, (dom + step) % 32)

        @pl.when(core == 0)
        def _():
            greet(level + 1, dom)

        @pl.when(core == 1)
        def _():
            from_dom = jnp.where(z_pos == 3, 7, 0) * 4 + x_pos
            greet((1 - half) * 8 + y_pos * 2, from_dom)
            greet((1 - half) * 8 + y_pos * 2 + 1, from_dom)

    for load in load_fine + load_mid:
        load.start()

    for load in load_small:
        load.wait()
    load_source.wait()
    lanes = lax.broadcasted_iota(jnp.int32, (1, 128), 1)
    for j in range(2):
        total = None
        for i in range(4):
            term = jnp.where(fine_map[i] == j, source[i], 0.0)
            total = term if total is None else total + term
        mid_g[j] = MID_WEIGHT * total
    wanted = jnp.where(lanes < 64, mid_map[0], mid_map[1])
    row = jnp.where((lanes % 64 < 16) & (lanes % 8 == wanted), 1.0, 0.0)
    for n in range(8):
        first = 4 * (n % 4) + 2 * (n // 4)
        for j in range(2):
            raw_out[n, 2 * j : 2 * j + 2, :] = mid_g[j, first : first + 2, :]
        raw_out[n, 4:5, :] = row

    def fill_halo(turn, fine_ref, mid_ref):
        halo_out[turn, 0] = fine_ref[fine_edges[0]]
        halo_out[turn, 1] = fine_ref[fine_edges[1]]
        halo_out[turn, 2] = mid_ref[mid_edges[0]]

    fill_halo(0, source, mid_g)

    @pl.when(dom == 0)
    def _():
        for turn in range(3):
            halo_in[turn, 0] = jnp.zeros((3, 16, 128), F32)

    @pl.when(dom == 31)
    def _():
        for turn in range(3):
            halo_in[turn, 1] = jnp.zeros((3, 16, 128), F32)

    @pl.when(centre)
    def _():
        raw_in[:, 5:8, :] = jnp.zeros((32, 3, 128), F32)

    sides = jnp.where(has_low, 1, 0) + jnp.where(has_high, 1, 0)
    waits = sides + 8 - centre_i + 3 + 63 * centre_i
    waits = waits + jnp.where(imports, 1, 0) + centre_i * core
    pl.semaphore_wait(barrier, waits)

    def halo_low(turn):
        return remote(
            halo_out.at[turn],
            halo_in.at[turn, 1],
            halo_send.at[turn, 0],
            halo_recv.at[turn, 1],
            level,
            dom - 1,
        )

    def halo_high(turn):
        return remote(
            halo_out.at[turn],
            halo_in.at[turn, 0],
            halo_send.at[turn, 1],
            halo_recv.at[turn, 0],
            level,
            dom + 1,
        )

    def start_halo(turn):
        @pl.when(has_low)
        def _():
            halo_low(turn).start()

        @pl.when(has_high)
        def _():
            halo_high(turn).start()

    def wait_halo(turn):
        @pl.when(has_low)
        def _():
            wait_for(halo_in.at[turn, 0], halo_recv.at[turn, 0])

        @pl.when(has_high)
        def _():
            wait_for(halo_in.at[turn, 1], halo_recv.at[turn, 1])

    raw_slot = raw_in.at[dom, pl.ds(0, 5)]
    for n in range(8):
        to_dom = (3 + n // 4) * 4 + n % 4

        @pl.when(to_dom != dom)
        def _():
            remote(raw_out.at[n], raw_slot, raw_send, raw_recv, level, to_dom).start()

        @pl.when(to_dom == dom)
        def _():
            pltpu.make_async_copy(raw_out.at[n], raw_slot, raw_recv).start()

    start_halo(0)

    @pl.when(centre & (core == 0))
    def _():
        pltpu.make_async_copy(inverse_hbm, inv_in.at[0], inv_recv).start()

    @pl.when(centre & (core == 1))
    def _():
        remote(inverse_hbm, inv_in.at[1], inv_send, inv_recv, level - 1, dom).start()

    @pl.when(imports)
    def _():
        remote(
            inverse_hbm,
            inv_in.at[core],
            inv_send,
            inv_recv,
            (1 - half) * 8 + y_pos * 2 + 1,
            import_z * 4 + x_pos,
        ).start()

    for r in range(4):
        load_fine[r].wait()
        for k in range(8):
            high, low = split(fine_raw[r, k])
            fine_w[r, 0:128, k * 128 : k * 128 + 128] = high
            fine_w[r, 128:256, k * 128 : k * 128 + 128] = low
    for r in range(2):
        load_mid[r].wait()
        for k in range(8):
            high, low = split(mid_raw[r, k])
            mid_w[r, 0:128, k * 128 : k * 128 + 128] = high
            mid_w[r, 128:256, k * 128 : k * 128 + 128] = low

    def put(ref, slot, value):
        high, low = split(value)
        ref[slot, 0:16, :] = high
        ref[slot, 16:32, :] = low

    constants = sweep_constants()

    def sweep(turn):
        keep, push = constants[turn]
        old_fine = source if turn == 0 else fine_e
        old_mid = mid_g if turn == 0 else mid_e
        old_fine_d = source if turn == 0 else fine_d
        old_mid_d = mid_g if turn == 0 else mid_d
        for r in range(4):
            put(fine_x, r, old_fine[r])
        for r in range(2):
            put(mid_x, r, old_mid[r])
        wait_halo(turn)
        for side in range(2):
            for row in range(2):
                put(fine_x, 4 + 2 * side + row, halo_in[turn, side, row])
            put(mid_x, 2 + side, halo_in[turn, side, 2])
        for r in range(4):
            left = jnp.concatenate([fine_x[fine_cols[r, k]] for k in range(8)], axis=1)
            applied = old_fine[r] + product(left, fine_w[r])
            step = keep * old_fine_d[r] + push * (source[r] - applied)
            fine_d[r] = step
            fine_e[r] = old_fine[r] + step
        for r in range(2):
            left = jnp.concatenate([mid_x[mid_cols[r, k]] for k in range(8)], axis=1)
            applied = old_mid[r] + product(left, mid_w[r])
            step = keep * old_mid_d[r] + push * (mid_g[r] - applied)
            mid_d[r] = step
            mid_e[r] = old_mid[r] + step
        if turn < 2:
            fill_halo(turn + 1, fine_e, mid_e)
            start_halo(turn + 1)


    @pl.when(centre)
    def _():
        wait_for(raw_in.at[:, pl.ds(0, 5)], raw_recv)
        rows = lax.broadcasted_iota(jnp.int32, (32, 8, 128), 1)
        cols = lax.broadcasted_iota(jnp.int32, (32, 8, 128), 2)
        value = raw_in[...]
        first = jnp.broadcast_to(value[:, 4:5, :], (32, 8, 128))
        second = pltpu.roll(first, 64, 2)
        picks = jnp.where(rows < 2, first, second)
        wanted = (rows < 4) & (cols // 8 == rows % 2)
        picks = jnp.where(wanted, picks, 0.0).reshape(256, 128).astype(BF16)
        high, low = split(value.reshape(256, 128))
        both = jnp.concatenate([high, low], axis=1)
        full = lax.dot_general(picks, both, (((0,), (0,)), ((), ())), preferred_element_type=F32)
        total = full[:16, :128] + full[:16, 128:]
        res_out[...] = total

        @pl.loop(0, 8)
        def _(peer):
            @pl.when(peer != mine)
            def _():
                remote(res_out, res_in.at[mine], res_send, res_recv, half * 8 + peer, dom).start()

            @pl.when(peer == mine)
            def _():
                pltpu.make_async_copy(res_out, res_in.at[mine], res_recv).start()

    sweep(0)

    @pl.when(centre)
    def _():
        wait_for(inv_in, inv_recv)
        for h in range(2):
            high, low = split(inv_in[h])
            inv_w[64 * h : 64 * h + 64, :] = high
            inv_w[128 + 64 * h : 192 + 64 * h, :] = low
        wait_for(res_in, res_recv)
        parts = []
        for c in range(8):
            block = jnp.concatenate([res_in[:, c, :], res_in[:, 8 + c, :]], axis=0)
            high, low = split(block)
            parts.append(jnp.concatenate([high, low], axis=0))
        left = jnp.concatenate(parts, axis=1)
        corr = product(left, inv_w[...])
        for peer in range(8):
            corr_out[peer, 0:1, :] = corr[peer : peer + 1, :]
            corr_out[peer, 1:2, :] = corr[8 + peer : 9 + peer, :]
        row = jnp.where(core == 0, half, 1 - half) * 4 + y_pos

        slot = final.at[x_pos, z_two, row]

        def result_to(peer, other_z):
            return remote(
                corr_out.at[peer],
                slot,
                z_send,
                z_recv.at[z_two],
                half * 8 + peer,
                other_z * 4 + x_pos,
            )

        @pl.loop(0, 7)
        def _(step):
            other_z = jnp.where(step % 2 == 0, step // 2, 7 - step // 2)
            other_z = jnp.where(other_z == z_pos, 7 - z_pos, other_z)
            for peer in range(8):
                result_to(peer, other_z).start()

        for peer in range(8):

            @pl.when(peer != mine)
            def _():
                result_to(peer, z_pos).start()

            @pl.when(peer == mine)
            def _():
                pltpu.make_async_copy(corr_out.at[peer], slot, z_recv.at[z_two]).start()

    sweep(1)
    sweep(2)
    for i in range(4):
        partial[i] = DAMPING * (fine_e[i] + MID_WEIGHT * mid_e[fine_map[i]])

    for which in range(2):
        wait_for(final.at[0, which], z_recv.at[which])
        for step in range(1, 4):
            remote(
                final.at[x_pos, which],
                final.at[x_pos, which],
                x_send,
                x_recv,
                level,
                z_pos * 4 + (x_pos + step) % 4,
            ).start()
    wait_for(final.at[pl.ds(0, 3)], x_recv)

    for j in range(2):
        for n in range(8):
            first = 4 * (n // 2) + 2 * (n % 2)
            picked[first : first + 2, :] = final[n // 2, n % 2, mid_map[j]]
        joined[j] = (DAMPING * MID_WEIGHT * COARSE_WEIGHT * COARSE_WEIGHT) * picked[...]
    for i in range(4):
        out[i] = partial[i] + joined[fine_map[i]]

    for turn in range(3):

        @pl.when(has_low)
        def _():
            wait_for(halo_out.at[turn], halo_send.at[turn, 0])

        @pl.when(has_high)
        def _():
            wait_for(halo_out.at[turn], halo_send.at[turn, 1])

    wait_for(final.at[pl.ds(0, 3)], x_send)

    @pl.when(imports | (centre & (core == 1)))
    def _():
        wait_for(inverse_hbm, inv_send)

    @pl.when(jnp.logical_not(centre))
    def _():
        wait_for(raw_out, raw_send)

    @pl.when(centre)
    def _():
        wait_for(raw_out.at[pl.ds(0, 7)], raw_send)
        wait_for(res_in.at[pl.ds(0, 7)], res_send)
        wait_for(spare, z_send)


def shards(
    right_side,
    fine_blocks,
    fine_cols,
    fine_edges,
    mid_blocks,
    mid_cols,
    mid_edges,
    fine_map,
    mid_map,
    coarse_inverse,
):
    hbm = pl.BlockSpec(memory_space=pltpu.HBM)
    smem = pltpu.SMEM
    vmem = pltpu.VMEM
    dma = pltpu.SemaphoreType.DMA
    return pl.pallas_call(
        kernel,
        out_shape=jax.ShapeDtypeStruct(right_side.shape, F32),
        in_specs=[hbm] * 10,
        out_specs=pl.BlockSpec(memory_space=vmem),
        scratch_shapes=[
            smem((4, 8), jnp.int32),
            smem((2,), jnp.int32),
            smem((2, 8), jnp.int32),
            smem((1,), jnp.int32),
            smem((4,), jnp.int32),
            smem((2,), jnp.int32),
            vmem((4, 16, 128), F32),
            vmem((4, 8, 128, 128), F32),
            vmem((2, 8, 128, 128), F32),
            vmem((4, 256, 1024), BF16),
            vmem((2, 256, 1024), BF16),
            vmem((4, 16, 128), F32),
            vmem((4, 16, 128), F32),
            vmem((2, 16, 128), F32),
            vmem((2, 16, 128), F32),
            vmem((2, 16, 128), F32),
            vmem((8, 32, 128), BF16),
            vmem((4, 32, 128), BF16),
            vmem((3, 3, 16, 128), F32),
            vmem((3, 2, 3, 16, 128), F32),
            vmem((8, 5, 128), F32),
            vmem((32, 8, 128), F32),
            vmem((16, 128), F32),
            vmem((8, 16, 128), F32),
            vmem((2, 64, 1024), F32),
            vmem((256, 1024), BF16),
            vmem((8, 2, 128), F32),
            vmem((63, 2, 128), F32),
            vmem((4, 2, 8, 2, 128), F32),
            vmem((16, 128), F32),
            vmem((2, 16, 128), F32),
            vmem((4, 16, 128), F32),
            dma((13,)),
            dma((3, 2)),
            dma((3, 2)),
            dma,
            dma,
            dma,
            dma,
            dma,
            dma,
            dma,
            dma((2,)),
            dma,
            dma,
        ],
        compiler_params=pltpu.CompilerParams(
            collective_id=0, has_side_effects=True, vmem_limit_bytes=40 * 1024 * 1024
        ),
    )(
        *[
            operand if operand is mid_edges else pltpu.with_memory_space_constraint(operand, pltpu.HBM)
            for operand in (
                fine_cols,
                fine_edges,
                mid_cols,
                mid_edges,
                fine_map,
                mid_map,
                right_side,
                fine_blocks,
                mid_blocks,
                coarse_inverse,
            )
        ]
    )


def solution(mesh):
    in_specs = (
        P("dom", "level", None),
        P("dom", None, None, None),
        P("dom", None),
        P("dom"),
        P("dom", None, None, None),
        P("dom", None),
        P("dom"),
        P("dom"),
        P("dom"),
        P("level", None),
    )
    out_specs = P("dom", "level", None)
    return jax.shard_map(shards, mesh=mesh, in_specs=in_specs, out_specs=out_specs, check_vma=False)
```

```python
import jax
import jax.numpy as jnp
from jax import lax
from jax.experimental import pallas as pl
from jax.experimental.pallas import tpu as pltpu
from jax.sharding import PartitionSpec as P

CAGG = 8
DEG = 4
CENTRE = 1.0
HALF_WIDTH = 0.7
DAMPING = 0.7
MID_WEIGHT = 0.5**0.5
COARSE_WEIGHT = CAGG**-0.5

F32 = jnp.float32
BF16 = jnp.bfloat16


def sweep_constants():
    ratio = CENTRE / HALF_WIDTH
    rho_prev = 1.0 / ratio
    constants = []
    for _ in range(DEG - 1):
        rho_next = 1.0 / (2.0 * ratio - rho_prev)
        constants.append((rho_next * rho_prev, 2.0 * rho_next / HALF_WIDTH))
        rho_prev = rho_next
    return constants


def split(value):
    high = value.astype(BF16)
    low = (value - high.astype(F32)).astype(BF16)
    return high, low


def product(left, right):
    full = lax.dot_general(left, right, (((1,), (1,)), ((), ())), preferred_element_type=F32)
    return full[:16, :128] + (full[:16, 128:] + full[16:, :128])


def wait_for(ref, sem):
    pltpu.make_async_copy(ref, ref, sem).wait()


def kernel(
    fine_cols_hbm,
    fine_edges_hbm,
    mid_cols_hbm,
    mid_edges_hbm,
    fine_map_hbm,
    mid_map_hbm,
    source_hbm,
    fine_hbm,
    mid_hbm,
    inverse_hbm,
    out,
    fine_cols,
    fine_edges,
    mid_cols,
    mid_edges,
    fine_map,
    mid_map,
    source,
    fine_raw,
    mid_raw,
    fine_w,
    mid_w,
    fine_e,
    fine_d,
    mid_g,
    mid_e,
    mid_d,
    fine_x,
    mid_x,
    halo_out,
    halo_in,
    raw_out,
    raw_in,
    res_out,
    res_in,
    inv_in,
    inv_w,
    corr_out,
    spare,
    final,
    picked,
    joined,
    partial,
    load_sem,
    halo_send,
    halo_recv,
    raw_send,
    raw_recv,
    inv_send,
    inv_recv,
    res_send,
    res_recv,
    z_send,
    z_recv,
    x_send,
    x_recv,
):
    level = lax.axis_index("level")
    dom = lax.axis_index("dom")
    half = level // 8
    mine = level % 8
    y_pos = mine // 2
    core = level % 2
    z_pos = dom // 4
    x_pos = dom % 4
    centre = (z_pos == 3) | (z_pos == 4)
    centre_i = jnp.where(centre, 1, 0)
    z_two = jnp.where(z_pos == 4, 1, 0)
    has_low = dom > 0
    has_high = dom < 31
    import_z = jnp.where(z_pos == 7, 3, 4)
    imports = (z_pos == 0) | (z_pos == 7)

    def remote(src, dst, send, recv, to_level, to_dom):
        return pltpu.make_async_remote_copy(
            src_ref=src,
            dst_ref=dst,
            send_sem=send,
            recv_sem=recv,
            device_id=(to_level, to_dom),
            device_id_type=pl.DeviceIdType.MESH,
        )

    barrier = pltpu.get_barrier_semaphore()

    def greet(to_level, to_dom):
        pl.semaphore_signal(
            barrier, inc=1, device_id=(to_level, to_dom), device_id_type=pl.DeviceIdType.MESH
        )

    @pl.when(centre)
    def _():
        for other_z in (7, 0, 6, 1, 5, 2, 4, 3):
            for other_x in range(4):

                @pl.when((z_pos != other_z) | (x_pos != other_x))
                def _():
                    greet(level, other_z * 4 + other_x)

        @pl.when(core == 0)
        def _():
            greet(level + 1, dom)

        @pl.when(core == 1)
        def _():
            from_dom = jnp.where(z_pos == 3, 7, 0) * 4 + x_pos
            greet((1 - half) * 8 + y_pos * 2, from_dom)
            greet((1 - half) * 8 + y_pos * 2 + 1, from_dom)

    load_small = [
        pltpu.make_async_copy(src, dst, load_sem.at[7 + n])
        for n, (src, dst) in enumerate(
            [
                (fine_map_hbm, fine_map),
                (mid_map_hbm, mid_map),
                (fine_edges_hbm, fine_edges),
                (mid_edges_hbm, mid_edges),
                (fine_cols_hbm, fine_cols),
                (mid_cols_hbm, mid_cols),
            ]
        )
    ]
    load_source = pltpu.make_async_copy(source_hbm, source, load_sem.at[0])
    for load in load_small[:2] + [load_source] + load_small[2:]:
        load.start()
    load_fine = [
        pltpu.make_async_copy(fine_hbm.at[r], fine_raw.at[r], load_sem.at[1 + r]) for r in range(4)
    ]
    load_mid = [
        pltpu.make_async_copy(mid_hbm.at[r], mid_raw.at[r], load_sem.at[5 + r]) for r in range(2)
    ]
    @pl.when(has_low)
    def _():
        greet(level, dom - 1)

    @pl.when(has_high)
    def _():
        greet(level, dom + 1)

    for step in range(1, 4):
        greet(level, z_pos * 4 + (x_pos + step) % 4)

    for other_z in (3, 4):
        for peer in range(8):

            @pl.when((z_pos != other_z) | (mine != peer))
            def _():
                greet(half * 8 + peer, other_z * 4 + x_pos)

    for load in load_fine + load_mid:
        load.start()

    for load in load_small:
        load.wait()
    load_source.wait()
    lanes = lax.broadcasted_iota(jnp.int32, (1, 128), 1)
    for j in range(2):
        total = None
        for i in range(4):
            term = jnp.where(fine_map[i] == j, source[i], 0.0)
            total = term if total is None else total + term
        mid_g[j] = MID_WEIGHT * total
    wanted = jnp.where(lanes < 64, mid_map[0], mid_map[1])
    row = jnp.where((lanes % 64 < 16) & (lanes % 8 == wanted), 1.0, 0.0)
    for n in range(8):
        first = 4 * (n % 4) + 2 * (n // 4)
        for j in range(2):
            raw_out[n, 2 * j : 2 * j + 2, :] = mid_g[j, first : first + 2, :]
        raw_out[n, 4:5, :] = row

    def fill_halo(turn, fine_ref, mid_ref):
        halo_out[turn, 0] = fine_ref[fine_edges[0]]
        halo_out[turn, 1] = fine_ref[fine_edges[1]]
        halo_out[turn, 2] = mid_ref[mid_edges[0]]

    fill_halo(0, source, mid_g)

    @pl.when(dom == 0)
    def _():
        for turn in range(3):
            halo_in[turn, 0] = jnp.zeros((3, 16, 128), F32)

    @pl.when(dom == 31)
    def _():
        for turn in range(3):
            halo_in[turn, 1] = jnp.zeros((3, 16, 128), F32)

    @pl.when(centre)
    def _():
        raw_in[:, 5:8, :] = jnp.zeros((32, 3, 128), F32)

    sides = jnp.where(has_low, 1, 0) + jnp.where(has_high, 1, 0)
    waits = sides + 8 - centre_i + 3 + 63 * centre_i
    waits = waits + jnp.where(imports, 1, 0) + centre_i * core
    pl.semaphore_wait(barrier, waits)

    def halo_low(turn):
        return remote(
            halo_out.at[turn],
            halo_in.at[turn, 1],
            halo_send.at[turn, 0],
            halo_recv.at[turn, 1],
            level,
            dom - 1,
        )

    def halo_high(turn):
        return remote(
            halo_out.at[turn],
            halo_in.at[turn, 0],
            halo_send.at[turn, 1],
            halo_recv.at[turn, 0],
            level,
            dom + 1,
        )

    def start_halo(turn):
        @pl.when(has_low)
        def _():
            halo_low(turn).start()

        @pl.when(has_high)
        def _():
            halo_high(turn).start()

    def wait_halo(turn):
        @pl.when(has_low)
        def _():
            wait_for(halo_in.at[turn, 0], halo_recv.at[turn, 0])

        @pl.when(has_high)
        def _():
            wait_for(halo_in.at[turn, 1], halo_recv.at[turn, 1])

    raw_slot = raw_in.at[dom, pl.ds(0, 5)]
    for n in range(8):
        to_dom = (3 + n // 4) * 4 + n % 4

        @pl.when(to_dom != dom)
        def _():
            remote(raw_out.at[n], raw_slot, raw_send, raw_recv, level, to_dom).start()

        @pl.when(to_dom == dom)
        def _():
            pltpu.make_async_copy(raw_out.at[n], raw_slot, raw_recv).start()

    start_halo(0)

    @pl.when(centre & (core == 0))
    def _():
        pltpu.make_async_copy(inverse_hbm, inv_in.at[0], inv_recv).start()

    @pl.when(centre & (core == 1))
    def _():
        remote(inverse_hbm, inv_in.at[1], inv_send, inv_recv, level - 1, dom).start()

    @pl.when(imports)
    def _():
        remote(
            inverse_hbm,
            inv_in.at[core],
            inv_send,
            inv_recv,
            (1 - half) * 8 + y_pos * 2 + 1,
            import_z * 4 + x_pos,
        ).start()

    for r in range(4):
        load_fine[r].wait()
        for k in range(8):
            high, low = split(fine_raw[r, k])
            fine_w[r, 0:128, k * 128 : k * 128 + 128] = high
            fine_w[r, 128:256, k * 128 : k * 128 + 128] = low
    for r in range(2):
        load_mid[r].wait()
        for k in range(8):
            high, low = split(mid_raw[r, k])
            mid_w[r, 0:128, k * 128 : k * 128 + 128] = high
            mid_w[r, 128:256, k * 128 : k * 128 + 128] = low

    def put(ref, slot, value):
        high, low = split(value)
        ref[slot, 0:16, :] = high
        ref[slot, 16:32, :] = low

    constants = sweep_constants()

    def sweep(turn):
        keep, push = constants[turn]
        old_fine = source if turn == 0 else fine_e
        old_mid = mid_g if turn == 0 else mid_e
        old_fine_d = source if turn == 0 else fine_d
        old_mid_d = mid_g if turn == 0 else mid_d
        for r in range(4):
            put(fine_x, r, old_fine[r])
        for r in range(2):
            put(mid_x, r, old_mid[r])
        wait_halo(turn)
        for side in range(2):
            for row in range(2):
                put(fine_x, 4 + 2 * side + row, halo_in[turn, side, row])
            put(mid_x, 2 + side, halo_in[turn, side, 2])
        for r in range(4):
            left = jnp.concatenate([fine_x[fine_cols[r, k]] for k in range(8)], axis=1)
            applied = old_fine[r] + product(left, fine_w[r])
            step = keep * old_fine_d[r] + push * (source[r] - applied)
            fine_d[r] = step
            fine_e[r] = old_fine[r] + step
        for r in range(2):
            left = jnp.concatenate([mid_x[mid_cols[r, k]] for k in range(8)], axis=1)
            applied = old_mid[r] + product(left, mid_w[r])
            step = keep * old_mid_d[r] + push * (mid_g[r] - applied)
            mid_d[r] = step
            mid_e[r] = old_mid[r] + step
        if turn < 2:
            fill_halo(turn + 1, fine_e, mid_e)
            start_halo(turn + 1)

    sweep(0)

    @pl.when(centre)
    def _():
        wait_for(raw_in.at[:, pl.ds(0, 5)], raw_recv)
        rows = lax.broadcasted_iota(jnp.int32, (32, 8, 128), 1)
        cols = lax.broadcasted_iota(jnp.int32, (32, 8, 128), 2)
        value = raw_in[...]
        first = jnp.broadcast_to(value[:, 4:5, :], (32, 8, 128))
        second = pltpu.roll(first, 64, 2)
        picks = jnp.where(rows < 2, first, second)
        wanted = (rows < 4) & (cols // 8 == rows % 2)
        picks = jnp.where(wanted, picks, 0.0).reshape(256, 128).astype(BF16)
        high, low = split(value.reshape(256, 128))
        both = jnp.concatenate([high, low], axis=1)
        full = lax.dot_general(picks, both, (((0,), (0,)), ((), ())), preferred_element_type=F32)
        total = full[:16, :128] + full[:16, 128:]
        res_out[...] = total

        @pl.loop(0, 8)
        def _(peer):
            @pl.when(peer != mine)
            def _():
                remote(res_out, res_in.at[mine], res_send, res_recv, half * 8 + peer, dom).start()

            @pl.when(peer == mine)
            def _():
                pltpu.make_async_copy(res_out, res_in.at[mine], res_recv).start()


    @pl.when(centre)
    def _():
        wait_for(inv_in, inv_recv)
        for h in range(2):
            high, low = split(inv_in[h])
            inv_w[64 * h : 64 * h + 64, :] = high
            inv_w[128 + 64 * h : 192 + 64 * h, :] = low
        wait_for(res_in, res_recv)
        parts = []
        for c in range(8):
            block = jnp.concatenate([res_in[:, c, :], res_in[:, 8 + c, :]], axis=0)
            high, low = split(block)
            parts.append(jnp.concatenate([high, low], axis=0))
        left = jnp.concatenate(parts, axis=1)
        corr = product(left, inv_w[...])
        for peer in range(8):
            corr_out[peer, 0:1, :] = corr[peer : peer + 1, :]
            corr_out[peer, 1:2, :] = corr[8 + peer : 9 + peer, :]
        row = jnp.where(core == 0, half, 1 - half) * 4 + y_pos

        slot = final.at[x_pos, z_two, row]

        def result_to(peer, other_z):
            return remote(
                corr_out.at[peer],
                slot,
                z_send,
                z_recv.at[z_two],
                half * 8 + peer,
                other_z * 4 + x_pos,
            )

        @pl.loop(0, 7)
        def _(step):
            other_z = jnp.where(step % 2 == 0, step // 2, 7 - step // 2)
            other_z = jnp.where(other_z == z_pos, 7 - z_pos, other_z)
            for peer in range(8):
                result_to(peer, other_z).start()

        for peer in range(8):

            @pl.when(peer != mine)
            def _():
                result_to(peer, z_pos).start()

            @pl.when(peer == mine)
            def _():
                pltpu.make_async_copy(corr_out.at[peer], slot, z_recv.at[z_two]).start()

    sweep(1)
    for which in range(2):
        wait_for(final.at[0, which], z_recv.at[which])
        for step in range(1, 4):
            remote(
                final.at[x_pos, which],
                final.at[x_pos, which],
                x_send,
                x_recv,
                level,
                z_pos * 4 + (x_pos + step) % 4,
            ).start()
    sweep(2)
    for i in range(4):
        partial[i] = DAMPING * (fine_e[i] + MID_WEIGHT * mid_e[fine_map[i]])

    wait_for(final.at[pl.ds(0, 3)], x_recv)

    for j in range(2):
        for n in range(8):
            first = 4 * (n // 2) + 2 * (n % 2)
            picked[first : first + 2, :] = final[n // 2, n % 2, mid_map[j]]
        joined[j] = (DAMPING * MID_WEIGHT * COARSE_WEIGHT * COARSE_WEIGHT) * picked[...]
    for i in range(4):
        out[i] = partial[i] + joined[fine_map[i]]

    for turn in range(3):

        @pl.when(has_low)
        def _():
            wait_for(halo_out.at[turn], halo_send.at[turn, 0])

        @pl.when(has_high)
        def _():
            wait_for(halo_out.at[turn], halo_send.at[turn, 1])

    wait_for(final.at[pl.ds(0, 3)], x_send)

    @pl.when(imports | (centre & (core == 1)))
    def _():
        wait_for(inverse_hbm, inv_send)

    @pl.when(jnp.logical_not(centre))
    def _():
        wait_for(raw_out, raw_send)

    @pl.when(centre)
    def _():
        wait_for(raw_out.at[pl.ds(0, 7)], raw_send)
        wait_for(res_in.at[pl.ds(0, 7)], res_send)
        wait_for(spare, z_send)


def shards(
    right_side,
    fine_blocks,
    fine_cols,
    fine_edges,
    mid_blocks,
    mid_cols,
    mid_edges,
    fine_map,
    mid_map,
    coarse_inverse,
):
    hbm = pl.BlockSpec(memory_space=pltpu.HBM)
    smem = pltpu.SMEM
    vmem = pltpu.VMEM
    dma = pltpu.SemaphoreType.DMA
    return pl.pallas_call(
        kernel,
        out_shape=jax.ShapeDtypeStruct(right_side.shape, F32),
        in_specs=[hbm] * 10,
        out_specs=pl.BlockSpec(memory_space=vmem),
        scratch_shapes=[
            smem((4, 8), jnp.int32),
            smem((2,), jnp.int32),
            smem((2, 8), jnp.int32),
            smem((1,), jnp.int32),
            smem((4,), jnp.int32),
            smem((2,), jnp.int32),
            vmem((4, 16, 128), F32),
            vmem((4, 8, 128, 128), F32),
            vmem((2, 8, 128, 128), F32),
            vmem((4, 256, 1024), BF16),
            vmem((2, 256, 1024), BF16),
            vmem((4, 16, 128), F32),
            vmem((4, 16, 128), F32),
            vmem((2, 16, 128), F32),
            vmem((2, 16, 128), F32),
            vmem((2, 16, 128), F32),
            vmem((8, 32, 128), BF16),
            vmem((4, 32, 128), BF16),
            vmem((3, 3, 16, 128), F32),
            vmem((3, 2, 3, 16, 128), F32),
            vmem((8, 5, 128), F32),
            vmem((32, 8, 128), F32),
            vmem((16, 128), F32),
            vmem((8, 16, 128), F32),
            vmem((2, 64, 1024), F32),
            vmem((256, 1024), BF16),
            vmem((8, 2, 128), F32),
            vmem((63, 2, 128), F32),
            vmem((4, 2, 8, 2, 128), F32),
            vmem((16, 128), F32),
            vmem((2, 16, 128), F32),
            vmem((4, 16, 128), F32),
            dma((13,)),
            dma((3, 2)),
            dma((3, 2)),
            dma,
            dma,
            dma,
            dma,
            dma,
            dma,
            dma,
            dma((2,)),
            dma,
            dma,
        ],
        compiler_params=pltpu.CompilerParams(
            collective_id=0, has_side_effects=True, vmem_limit_bytes=40 * 1024 * 1024
        ),
    )(
        *[
            operand if operand is mid_edges else pltpu.with_memory_space_constraint(operand, pltpu.HBM)
            for operand in (
                fine_cols,
                fine_edges,
                mid_cols,
                mid_edges,
                fine_map,
                mid_map,
                right_side,
                fine_blocks,
                mid_blocks,
                coarse_inverse,
            )
        ]
    )


def solution(mesh):
    in_specs = (
        P("dom", "level", None),
        P("dom", None, None, None),
        P("dom", None),
        P("dom"),
        P("dom", None, None, None),
        P("dom", None),
        P("dom"),
        P("dom"),
        P("dom"),
        P("level", None),
    )
    out_specs = P("dom", "level", None)
    return jax.shard_map(shards, mesh=mesh, in_specs=in_specs, out_specs=out_specs, check_vma=False)
```

```python
import jax
import jax.numpy as jnp
from jax import lax
from jax.experimental import pallas as pl
from jax.experimental.pallas import tpu as pltpu
from jax.sharding import PartitionSpec as P

CAGG = 8
DEG = 4
CENTRE = 1.0
HALF_WIDTH = 0.7
DAMPING = 0.7
MID_WEIGHT = 0.5**0.5
COARSE_WEIGHT = CAGG**-0.5

F32 = jnp.float32
BF16 = jnp.bfloat16


def sweep_constants():
    ratio = CENTRE / HALF_WIDTH
    rho_prev = 1.0 / ratio
    constants = []
    for _ in range(DEG - 1):
        rho_next = 1.0 / (2.0 * ratio - rho_prev)
        constants.append((rho_next * rho_prev, 2.0 * rho_next / HALF_WIDTH))
        rho_prev = rho_next
    return constants


def split(value):
    high = value.astype(BF16)
    low = (value - high.astype(F32)).astype(BF16)
    return high, low


def product(left, right):
    full = lax.dot_general(left, right, (((1,), (1,)), ((), ())), preferred_element_type=F32)
    return full[:16, :128] + (full[:16, 128:] + full[16:, :128])


def wait_for(ref, sem):
    pltpu.make_async_copy(ref, ref, sem).wait()


def kernel(
    fine_cols_hbm,
    fine_edges_hbm,
    mid_cols_hbm,
    mid_edges_hbm,
    fine_map_hbm,
    mid_map_hbm,
    source_hbm,
    fine_hbm,
    mid_hbm,
    inverse_hbm,
    out,
    fine_cols,
    fine_edges,
    mid_cols,
    mid_edges,
    fine_map,
    mid_map,
    source,
    fine_raw,
    mid_raw,
    fine_w,
    mid_w,
    fine_e,
    fine_d,
    mid_g,
    mid_e,
    mid_d,
    fine_x,
    mid_x,
    halo_out,
    halo_in,
    raw_out,
    raw_in,
    res_out,
    res_in,
    inv_in,
    inv_w,
    corr_out,
    spare,
    final,
    picked,
    joined,
    partial,
    load_sem,
    halo_send,
    halo_recv,
    raw_send,
    raw_recv,
    inv_send,
    inv_recv,
    res_send,
    res_recv,
    z_send,
    early_send,
    z_recv,
    x_send,
    x_recv,
):
    level = lax.axis_index("level")
    dom = lax.axis_index("dom")
    half = level // 8
    mine = level % 8
    y_pos = mine // 2
    core = level % 2
    z_pos = dom // 4
    x_pos = dom % 4
    centre = (z_pos == 3) | (z_pos == 4)
    centre_i = jnp.where(centre, 1, 0)
    z_two = jnp.where(z_pos == 4, 1, 0)
    has_low = dom > 0
    has_high = dom < 31
    early = (half == 0) & (z_pos == 0)
    import_z = jnp.where(z_pos == 7, 3, 4)
    imports = (z_pos == 0) | (z_pos == 7)

    def remote(src, dst, send, recv, to_level, to_dom):
        return pltpu.make_async_remote_copy(
            src_ref=src,
            dst_ref=dst,
            send_sem=send,
            recv_sem=recv,
            device_id=(to_level, to_dom),
            device_id_type=pl.DeviceIdType.MESH,
        )

    barrier = pltpu.get_barrier_semaphore()

    def greet(to_level, to_dom):
        pl.semaphore_signal(
            barrier, inc=1, device_id=(to_level, to_dom), device_id_type=pl.DeviceIdType.MESH
        )

    @pl.when(centre)
    def _():
        for other_z in (7, 0, 6, 1, 5, 2, 4, 3):
            for other_x in range(4):

                @pl.when((z_pos != other_z) | (x_pos != other_x))
                def _():
                    greet(level, other_z * 4 + other_x)

        @pl.when(core == 0)
        def _():
            greet(level + 1, dom)

        @pl.when(core == 1)
        def _():
            from_dom = jnp.where(z_pos == 3, 7, 0) * 4 + x_pos
            greet((1 - half) * 8 + y_pos * 2, from_dom)
            greet((1 - half) * 8 + y_pos * 2 + 1, from_dom)

    load_small = [
        pltpu.make_async_copy(src, dst, load_sem.at[7 + n])
        for n, (src, dst) in enumerate(
            [
                (fine_map_hbm, fine_map),
                (mid_map_hbm, mid_map),
                (fine_edges_hbm, fine_edges),
                (mid_edges_hbm, mid_edges),
                (fine_cols_hbm, fine_cols),
                (mid_cols_hbm, mid_cols),
            ]
        )
    ]
    load_source = pltpu.make_async_copy(source_hbm, source, load_sem.at[0])
    for load in load_small[:2] + [load_source] + load_small[2:]:
        load.start()
    load_fine = [
        pltpu.make_async_copy(fine_hbm.at[r], fine_raw.at[r], load_sem.at[1 + r]) for r in range(4)
    ]
    load_mid = [
        pltpu.make_async_copy(mid_hbm.at[r], mid_raw.at[r], load_sem.at[5 + r]) for r in range(2)
    ]
    @pl.when(has_low)
    def _():
        greet(level, dom - 1)

    @pl.when(has_high)
    def _():
        greet(level, dom + 1)

    @pl.when(jnp.logical_not(early))
    def _():
        for step in range(1, 4):
            greet(level, z_pos * 4 + (x_pos + step) % 4)

    for other_z in (3, 4):
        for peer in range(8):

            @pl.when((z_pos != other_z) | (mine != peer))
            def _():
                greet(half * 8 + peer, other_z * 4 + x_pos)

    @pl.when(early)
    def _():
        for step in range(1, 4):
            for other_z in (3, 4):
                for peer in range(8):
                    greet(peer, other_z * 4 + (x_pos + step) % 4)

    for load in load_fine + load_mid:
        load.start()

    for load in load_small:
        load.wait()
    load_source.wait()
    lanes = lax.broadcasted_iota(jnp.int32, (1, 128), 1)
    for j in range(2):
        total = None
        for i in range(4):
            term = jnp.where(fine_map[i] == j, source[i], 0.0)
            total = term if total is None else total + term
        mid_g[j] = MID_WEIGHT * total
    wanted = jnp.where(lanes < 64, mid_map[0], mid_map[1])
    row = jnp.where((lanes % 64 < 16) & (lanes % 8 == wanted), 1.0, 0.0)
    for n in range(8):
        first = 4 * (n % 4) + 2 * (n // 4)
        for j in range(2):
            raw_out[n, 2 * j : 2 * j + 2, :] = mid_g[j, first : first + 2, :]
        raw_out[n, 4:5, :] = row

    def fill_halo(turn, fine_ref, mid_ref):
        halo_out[turn, 0] = fine_ref[fine_edges[0]]
        halo_out[turn, 1] = fine_ref[fine_edges[1]]
        halo_out[turn, 2] = mid_ref[mid_edges[0]]

    fill_halo(0, source, mid_g)

    @pl.when(dom == 0)
    def _():
        for turn in range(3):
            halo_in[turn, 0] = jnp.zeros((3, 16, 128), F32)

    @pl.when(dom == 31)
    def _():
        for turn in range(3):
            halo_in[turn, 1] = jnp.zeros((3, 16, 128), F32)

    @pl.when(centre)
    def _():
        raw_in[:, 5:8, :] = jnp.zeros((32, 3, 128), F32)

    sides = jnp.where(has_low, 1, 0) + jnp.where(has_high, 1, 0)
    waits = sides + 8 - centre_i + 3 + 63 * centre_i
    waits = waits + jnp.where(centre & (half == 0), 24, 0) - jnp.where(early, 3, 0)
    waits = waits + jnp.where(imports, 1, 0) + centre_i * core
    pl.semaphore_wait(barrier, waits)

    def halo_low(turn):
        return remote(
            halo_out.at[turn],
            halo_in.at[turn, 1],
            halo_send.at[turn, 0],
            halo_recv.at[turn, 1],
            level,
            dom - 1,
        )

    def halo_high(turn):
        return remote(
            halo_out.at[turn],
            halo_in.at[turn, 0],
            halo_send.at[turn, 1],
            halo_recv.at[turn, 0],
            level,
            dom + 1,
        )

    def start_halo(turn):
        @pl.when(has_low)
        def _():
            halo_low(turn).start()

        @pl.when(has_high)
        def _():
            halo_high(turn).start()

    def wait_halo(turn):
        @pl.when(has_low)
        def _():
            wait_for(halo_in.at[turn, 0], halo_recv.at[turn, 0])

        @pl.when(has_high)
        def _():
            wait_for(halo_in.at[turn, 1], halo_recv.at[turn, 1])

    raw_slot = raw_in.at[dom, pl.ds(0, 5)]
    for n in range(8):
        to_dom = (3 + n // 4) * 4 + n % 4

        @pl.when(to_dom != dom)
        def _():
            remote(raw_out.at[n], raw_slot, raw_send, raw_recv, level, to_dom).start()

        @pl.when(to_dom == dom)
        def _():
            pltpu.make_async_copy(raw_out.at[n], raw_slot, raw_recv).start()

    start_halo(0)

    @pl.when(centre & (core == 0))
    def _():
        pltpu.make_async_copy(inverse_hbm, inv_in.at[0], inv_recv).start()

    @pl.when(centre & (core == 1))
    def _():
        remote(inverse_hbm, inv_in.at[1], inv_send, inv_recv, level - 1, dom).start()

    @pl.when(imports)
    def _():
        remote(
            inverse_hbm,
            inv_in.at[core],
            inv_send,
            inv_recv,
            (1 - half) * 8 + y_pos * 2 + 1,
            import_z * 4 + x_pos,
        ).start()

    for r in range(4):
        load_fine[r].wait()
        for k in range(8):
            high, low = split(fine_raw[r, k])
            fine_w[r, 0:128, k * 128 : k * 128 + 128] = high
            fine_w[r, 128:256, k * 128 : k * 128 + 128] = low
    for r in range(2):
        load_mid[r].wait()
        for k in range(8):
            high, low = split(mid_raw[r, k])
            mid_w[r, 0:128, k * 128 : k * 128 + 128] = high
            mid_w[r, 128:256, k * 128 : k * 128 + 128] = low

    def put(ref, slot, value):
        high, low = split(value)
        ref[slot, 0:16, :] = high
        ref[slot, 16:32, :] = low

    constants = sweep_constants()

    def sweep(turn):
        keep, push = constants[turn]
        old_fine = source if turn == 0 else fine_e
        old_mid = mid_g if turn == 0 else mid_e
        old_fine_d = source if turn == 0 else fine_d
        old_mid_d = mid_g if turn == 0 else mid_d
        for r in range(4):
            put(fine_x, r, old_fine[r])
        for r in range(2):
            put(mid_x, r, old_mid[r])
        wait_halo(turn)
        for side in range(2):
            for row in range(2):
                put(fine_x, 4 + 2 * side + row, halo_in[turn, side, row])
            put(mid_x, 2 + side, halo_in[turn, side, 2])
        for r in range(4):
            left = jnp.concatenate([fine_x[fine_cols[r, k]] for k in range(8)], axis=1)
            applied = old_fine[r] + product(left, fine_w[r])
            step = keep * old_fine_d[r] + push * (source[r] - applied)
            fine_d[r] = step
            fine_e[r] = old_fine[r] + step
        for r in range(2):
            left = jnp.concatenate([mid_x[mid_cols[r, k]] for k in range(8)], axis=1)
            applied = old_mid[r] + product(left, mid_w[r])
            step = keep * old_mid_d[r] + push * (mid_g[r] - applied)
            mid_d[r] = step
            mid_e[r] = old_mid[r] + step
        if turn < 2:
            fill_halo(turn + 1, fine_e, mid_e)
            start_halo(turn + 1)

    sweep(0)

    @pl.when(centre)
    def _():
        wait_for(raw_in.at[:, pl.ds(0, 5)], raw_recv)
        rows = lax.broadcasted_iota(jnp.int32, (32, 8, 128), 1)
        cols = lax.broadcasted_iota(jnp.int32, (32, 8, 128), 2)
        value = raw_in[...]
        first = jnp.broadcast_to(value[:, 4:5, :], (32, 8, 128))
        second = pltpu.roll(first, 64, 2)
        picks = jnp.where(rows < 2, first, second)
        wanted = (rows < 4) & (cols // 8 == rows % 2)
        picks = jnp.where(wanted, picks, 0.0).reshape(256, 128).astype(BF16)
        high, low = split(value.reshape(256, 128))
        both = jnp.concatenate([high, low], axis=1)
        full = lax.dot_general(picks, both, (((0,), (0,)), ((), ())), preferred_element_type=F32)
        total = full[:16, :128] + full[:16, 128:]
        res_out[...] = total

        @pl.loop(0, 8)
        def _(peer):
            @pl.when(peer != mine)
            def _():
                remote(res_out, res_in.at[mine], res_send, res_recv, half * 8 + peer, dom).start()

            @pl.when(peer == mine)
            def _():
                pltpu.make_async_copy(res_out, res_in.at[mine], res_recv).start()


    @pl.when(centre)
    def _():
        wait_for(inv_in, inv_recv)
        for h in range(2):
            high, low = split(inv_in[h])
            inv_w[64 * h : 64 * h + 64, :] = high
            inv_w[128 + 64 * h : 192 + 64 * h, :] = low
        wait_for(res_in, res_recv)
        parts = []
        for c in range(8):
            block = jnp.concatenate([res_in[:, c, :], res_in[:, 8 + c, :]], axis=0)
            high, low = split(block)
            parts.append(jnp.concatenate([high, low], axis=0))
        left = jnp.concatenate(parts, axis=1)
        corr = product(left, inv_w[...])
        for peer in range(8):
            corr_out[peer, 0:1, :] = corr[peer : peer + 1, :]
            corr_out[peer, 1:2, :] = corr[8 + peer : 9 + peer, :]
        row = jnp.where(core == 0, half, 1 - half) * 4 + y_pos

        slot = final.at[x_pos, z_two, row]

        def result_to(peer, other_z):
            return remote(
                corr_out.at[peer],
                slot,
                z_send,
                z_recv.at[z_two],
                half * 8 + peer,
                other_z * 4 + x_pos,
            )

        @pl.when(half == 0)
        def _():
            @pl.loop(1, 4)
            def _(step):
                for peer in range(8):
                    remote(
                        corr_out.at[peer],
                        slot,
                        early_send,
                        z_recv.at[z_two],
                        peer,
                        (x_pos + step) % 4,
                    ).start()

        for first_half, second_half in ((0, 7), (1, 0), (2, 6), (7, 1), (6, 5), (5, 2)):
            for peer in range(8):
                result_to(peer, jnp.where(half == 0, first_half, second_half)).start()
        for peer in range(8):
            result_to(peer, 7 - z_pos).start()

        for peer in range(8):

            @pl.when(peer != mine)
            def _():
                result_to(peer, z_pos).start()

            @pl.when(peer == mine)
            def _():
                pltpu.make_async_copy(corr_out.at[peer], slot, z_recv.at[z_two]).start()

    sweep(1)
    @pl.when(jnp.logical_not(early))
    def _():
        for which in range(2):
            wait_for(final.at[0, which], z_recv.at[which])
            for step in range(1, 4):
                remote(
                    final.at[x_pos, which],
                    final.at[x_pos, which],
                    x_send,
                    x_recv,
                    level,
                    z_pos * 4 + (x_pos + step) % 4,
                ).start()

    sweep(2)
    for i in range(4):
        partial[i] = DAMPING * (fine_e[i] + MID_WEIGHT * mid_e[fine_map[i]])

    @pl.when(early)
    def _():
        for which in range(2):
            wait_for(final.at[pl.ds(0, 2)], z_recv.at[which])

    @pl.when(jnp.logical_not(early))
    def _():
        wait_for(final.at[pl.ds(0, 3)], x_recv)

    for j in range(2):
        for n in range(8):
            first = 4 * (n // 2) + 2 * (n % 2)
            picked[first : first + 2, :] = final[n // 2, n % 2, mid_map[j]]
        joined[j] = (DAMPING * MID_WEIGHT * COARSE_WEIGHT * COARSE_WEIGHT) * picked[...]
    for i in range(4):
        out[i] = partial[i] + joined[fine_map[i]]

    for turn in range(3):

        @pl.when(has_low)
        def _():
            wait_for(halo_out.at[turn], halo_send.at[turn, 0])

        @pl.when(has_high)
        def _():
            wait_for(halo_out.at[turn], halo_send.at[turn, 1])

    @pl.when(jnp.logical_not(early))
    def _():
        wait_for(final.at[pl.ds(0, 3)], x_send)

    @pl.when(imports | (centre & (core == 1)))
    def _():
        wait_for(inverse_hbm, inv_send)

    @pl.when(jnp.logical_not(centre))
    def _():
        wait_for(raw_out, raw_send)

    @pl.when(centre)
    def _():
        wait_for(raw_out.at[pl.ds(0, 7)], raw_send)
        wait_for(res_in.at[pl.ds(0, 7)], res_send)
        wait_for(spare, z_send)

        @pl.when(half == 0)
        def _():
            wait_for(spare.at[pl.ds(0, 24)], early_send)


def shards(
    right_side,
    fine_blocks,
    fine_cols,
    fine_edges,
    mid_blocks,
    mid_cols,
    mid_edges,
    fine_map,
    mid_map,
    coarse_inverse,
):
    hbm = pl.BlockSpec(memory_space=pltpu.HBM)
    smem = pltpu.SMEM
    vmem = pltpu.VMEM
    dma = pltpu.SemaphoreType.DMA
    return pl.pallas_call(
        kernel,
        out_shape=jax.ShapeDtypeStruct(right_side.shape, F32),
        in_specs=[hbm] * 10,
        out_specs=pl.BlockSpec(memory_space=vmem),
        scratch_shapes=[
            smem((4, 8), jnp.int32),
            smem((2,), jnp.int32),
            smem((2, 8), jnp.int32),
            smem((1,), jnp.int32),
            smem((4,), jnp.int32),
            smem((2,), jnp.int32),
            vmem((4, 16, 128), F32),
            vmem((4, 8, 128, 128), F32),
            vmem((2, 8, 128, 128), F32),
            vmem((4, 256, 1024), BF16),
            vmem((2, 256, 1024), BF16),
            vmem((4, 16, 128), F32),
            vmem((4, 16, 128), F32),
            vmem((2, 16, 128), F32),
            vmem((2, 16, 128), F32),
            vmem((2, 16, 128), F32),
            vmem((8, 32, 128), BF16),
            vmem((4, 32, 128), BF16),
            vmem((3, 3, 16, 128), F32),
            vmem((3, 2, 3, 16, 128), F32),
            vmem((8, 5, 128), F32),
            vmem((32, 8, 128), F32),
            vmem((16, 128), F32),
            vmem((8, 16, 128), F32),
            vmem((2, 64, 1024), F32),
            vmem((256, 1024), BF16),
            vmem((8, 2, 128), F32),
            vmem((63, 2, 128), F32),
            vmem((4, 2, 8, 2, 128), F32),
            vmem((16, 128), F32),
            vmem((2, 16, 128), F32),
            vmem((4, 16, 128), F32),
            dma((13,)),
            dma((3, 2)),
            dma((3, 2)),
            dma,
            dma,
            dma,
            dma,
            dma,
            dma,
            dma,
            dma,
            dma((2,)),
            dma,
            dma,
        ],
        compiler_params=pltpu.CompilerParams(
            collective_id=0, has_side_effects=True, vmem_limit_bytes=40 * 1024 * 1024
        ),
    )(
        *[
            operand if operand is mid_edges else pltpu.with_memory_space_constraint(operand, pltpu.HBM)
            for operand in (
                fine_cols,
                fine_edges,
                mid_cols,
                mid_edges,
                fine_map,
                mid_map,
                right_side,
                fine_blocks,
                mid_blocks,
                coarse_inverse,
            )
        ]
    )


def solution(mesh):
    in_specs = (
        P("dom", "level", None),
        P("dom", None, None, None),
        P("dom", None),
        P("dom"),
        P("dom", None, None, None),
        P("dom", None),
        P("dom"),
        P("dom"),
        P("dom"),
        P("level", None),
    )
    out_specs = P("dom", "level", None)
    return jax.shard_map(shards, mesh=mesh, in_specs=in_specs, out_specs=out_specs, check_vma=False)
```

```python
import jax
import jax.numpy as jnp
from jax import lax
from jax.experimental import pallas as pl
from jax.experimental.pallas import tpu as pltpu
from jax.sharding import PartitionSpec as P

CAGG = 8
DEG = 4
CENTRE = 1.0
HALF_WIDTH = 0.7
DAMPING = 0.7
MID_WEIGHT = 0.5**0.5
COARSE_WEIGHT = CAGG**-0.5

F32 = jnp.float32
BF16 = jnp.bfloat16


def sweep_constants():
    ratio = CENTRE / HALF_WIDTH
    rho_prev = 1.0 / ratio
    constants = []
    for _ in range(DEG - 1):
        rho_next = 1.0 / (2.0 * ratio - rho_prev)
        constants.append((rho_next * rho_prev, 2.0 * rho_next / HALF_WIDTH))
        rho_prev = rho_next
    return constants


def split(value):
    high = value.astype(BF16)
    low = (value - high.astype(F32)).astype(BF16)
    return high, low


def product(left, right):
    full = lax.dot_general(left, right, (((1,), (1,)), ((), ())), preferred_element_type=F32)
    return full[:16, :128] + (full[:16, 128:] + full[16:, :128])


def wait_for(ref, sem):
    pltpu.make_async_copy(ref, ref, sem).wait()


def kernel(
    fine_cols_hbm,
    fine_edges_hbm,
    mid_cols_hbm,
    mid_edges_hbm,
    fine_map_hbm,
    mid_map_hbm,
    source_hbm,
    fine_hbm,
    mid_hbm,
    inverse_hbm,
    out,
    fine_cols,
    fine_edges,
    mid_cols,
    mid_edges,
    fine_map,
    mid_map,
    source,
    fine_raw,
    mid_raw,
    fine_w,
    mid_w,
    fine_e,
    fine_d,
    mid_g,
    mid_e,
    mid_d,
    fine_x,
    mid_x,
    halo_out,
    halo_in,
    raw_out,
    raw_in,
    res_out,
    res_in,
    inv_in,
    inv_w,
    corr_out,
    spare,
    final,
    picked,
    joined,
    partial,
    load_sem,
    halo_send,
    halo_recv,
    raw_send,
    raw_recv,
    inv_send,
    inv_recv,
    res_send,
    res_recv,
    z_send,
    early_send,
    z_recv,
    x_send,
    x_recv,
):
    level = lax.axis_index("level")
    dom = lax.axis_index("dom")
    half = level // 8
    mine = level % 8
    y_pos = mine // 2
    core = level % 2
    z_pos = dom // 4
    x_pos = dom % 4
    centre = (z_pos == 3) | (z_pos == 4)
    centre_i = jnp.where(centre, 1, 0)
    z_two = jnp.where(z_pos == 4, 1, 0)
    has_low = dom > 0
    has_high = dom < 31
    early = (half == 0) & (z_pos == 0)
    import_z = jnp.where(z_pos == 7, 3, 4)
    imports = (z_pos == 0) | (z_pos == 7)

    def remote(src, dst, send, recv, to_level, to_dom):
        return pltpu.make_async_remote_copy(
            src_ref=src,
            dst_ref=dst,
            send_sem=send,
            recv_sem=recv,
            device_id=(to_level, to_dom),
            device_id_type=pl.DeviceIdType.MESH,
        )

    barrier = pltpu.get_barrier_semaphore()

    def greet(to_level, to_dom):
        pl.semaphore_signal(
            barrier, inc=1, device_id=(to_level, to_dom), device_id_type=pl.DeviceIdType.MESH
        )

    @pl.when(centre)
    def _():
        for other_z in (7, 0, 6, 1, 5, 2, 4, 3):
            for other_x in range(4):

                @pl.when((z_pos != other_z) | (x_pos != other_x))
                def _():
                    greet(level, other_z * 4 + other_x)

        @pl.when(core == 0)
        def _():
            greet(level + 1, dom)

        @pl.when(core == 1)
        def _():
            from_dom = jnp.where(z_pos == 3, 7, 0) * 4 + x_pos
            greet((1 - half) * 8 + y_pos * 2, from_dom)
            greet((1 - half) * 8 + y_pos * 2 + 1, from_dom)

    load_small = [
        pltpu.make_async_copy(src, dst, load_sem.at[7 + n])
        for n, (src, dst) in enumerate(
            [
                (fine_map_hbm, fine_map),
                (mid_map_hbm, mid_map),
                (fine_edges_hbm, fine_edges),
                (mid_edges_hbm, mid_edges),
                (fine_cols_hbm, fine_cols),
                (mid_cols_hbm, mid_cols),
            ]
        )
    ]
    load_source = pltpu.make_async_copy(source_hbm, source, load_sem.at[0])
    for load in load_small[:2] + [load_source] + load_small[2:]:
        load.start()
    load_fine = [
        pltpu.make_async_copy(fine_hbm.at[r], fine_raw.at[r], load_sem.at[1 + r]) for r in range(4)
    ]
    load_mid = [
        pltpu.make_async_copy(mid_hbm.at[r], mid_raw.at[r], load_sem.at[5 + r]) for r in range(2)
    ]
    @pl.when(has_low)
    def _():
        greet(level, dom - 1)

    @pl.when(has_high)
    def _():
        greet(level, dom + 1)

    @pl.when(jnp.logical_not(early))
    def _():
        for step in range(1, 4):
            greet(level, z_pos * 4 + (x_pos + step) % 4)

    for other_z in (3, 4):
        for peer in range(8):

            @pl.when((z_pos != other_z) | (mine != peer))
            def _():
                greet(half * 8 + peer, other_z * 4 + x_pos)

    @pl.when(early)
    def _():
        for step in range(1, 4):
            for other_z in (3, 4):
                for peer in range(8):
                    greet(peer, other_z * 4 + (x_pos + step) % 4)

    for load in load_fine + load_mid:
        load.start()

    for load in load_small:
        load.wait()
    load_source.wait()
    lanes = lax.broadcasted_iota(jnp.int32, (1, 128), 1)
    for j in range(2):
        total = None
        for i in range(4):
            term = jnp.where(fine_map[i] == j, source[i], 0.0)
            total = term if total is None else total + term
        mid_g[j] = MID_WEIGHT * total
    wanted = jnp.where(lanes < 64, mid_map[0], mid_map[1])
    row = jnp.where((lanes % 64 < 16) & (lanes % 8 == wanted), 1.0, 0.0)
    for n in range(8):
        first = 4 * (n % 4) + 2 * (n // 4)
        for j in range(2):
            raw_out[n, 2 * j : 2 * j + 2, :] = mid_g[j, first : first + 2, :]
        raw_out[n, 4:5, :] = row

    def fill_halo(turn, fine_ref, mid_ref):
        halo_out[turn, 0] = fine_ref[fine_edges[0]]
        halo_out[turn, 1] = fine_ref[fine_edges[1]]
        halo_out[turn, 2] = mid_ref[mid_edges[0]]

    fill_halo(0, source, mid_g)

    @pl.when(dom == 0)
    def _():
        for turn in range(3):
            halo_in[turn, 0] = jnp.zeros((3, 16, 128), F32)

    @pl.when(dom == 31)
    def _():
        for turn in range(3):
            halo_in[turn, 1] = jnp.zeros((3, 16, 128), F32)

    @pl.when(centre)
    def _():
        raw_in[:, 5:8, :] = jnp.zeros((32, 3, 128), F32)

    sides = jnp.where(has_low, 1, 0) + jnp.where(has_high, 1, 0)
    waits = sides + 8 - centre_i + 3 + 63 * centre_i
    waits = waits + jnp.where(centre & (half == 0), 24, 0) - jnp.where(early, 3, 0)
    waits = waits + jnp.where(imports, 1, 0) + centre_i * core
    pl.semaphore_wait(barrier, waits)

    def halo_low(turn):
        return remote(
            halo_out.at[turn],
            halo_in.at[turn, 1],
            halo_send.at[turn, 0],
            halo_recv.at[turn, 1],
            level,
            dom - 1,
        )

    def halo_high(turn):
        return remote(
            halo_out.at[turn],
            halo_in.at[turn, 0],
            halo_send.at[turn, 1],
            halo_recv.at[turn, 0],
            level,
            dom + 1,
        )

    def start_halo(turn):
        @pl.when(has_low)
        def _():
            halo_low(turn).start()

        @pl.when(has_high)
        def _():
            halo_high(turn).start()

    def wait_halo(turn):
        @pl.when(has_low)
        def _():
            wait_for(halo_in.at[turn, 0], halo_recv.at[turn, 0])

        @pl.when(has_high)
        def _():
            wait_for(halo_in.at[turn, 1], halo_recv.at[turn, 1])

    raw_slot = raw_in.at[dom, pl.ds(0, 5)]
    far = jnp.where(z_pos < 4, 1, 0)
    for step, near in ((2, 0), (1, 0), (3, 0), (2, 1), (0, 0), (1, 1), (3, 1)):
        which = jnp.where(near == 1, 1 - far, far)
        to_x = (x_pos + step) % 4
        to_dom = (3 + which) * 4 + to_x
        remote(
            raw_out.at[which * 4 + to_x], raw_slot, raw_send, raw_recv, level, to_dom
        ).start()
    last = raw_out.at[(1 - far) * 4 + x_pos]

    @pl.when(jnp.logical_not(centre))
    def _():
        remote(last, raw_slot, raw_send, raw_recv, level, (4 - far) * 4 + x_pos).start()

    @pl.when(centre)
    def _():
        pltpu.make_async_copy(last, raw_slot, raw_recv).start()

    start_halo(0)

    @pl.when(centre & (core == 0))
    def _():
        pltpu.make_async_copy(inverse_hbm, inv_in.at[0], inv_recv).start()

    @pl.when(centre & (core == 1))
    def _():
        remote(inverse_hbm, inv_in.at[1], inv_send, inv_recv, level - 1, dom).start()

    @pl.when(imports)
    def _():
        remote(
            inverse_hbm,
            inv_in.at[core],
            inv_send,
            inv_recv,
            (1 - half) * 8 + y_pos * 2 + 1,
            import_z * 4 + x_pos,
        ).start()

    for r in range(4):
        load_fine[r].wait()
        for k in range(8):
            high, low = split(fine_raw[r, k])
            fine_w[r, 0:128, k * 128 : k * 128 + 128] = high
            fine_w[r, 128:256, k * 128 : k * 128 + 128] = low
    for r in range(2):
        load_mid[r].wait()
        for k in range(8):
            high, low = split(mid_raw[r, k])
            mid_w[r, 0:128, k * 128 : k * 128 + 128] = high
            mid_w[r, 128:256, k * 128 : k * 128 + 128] = low

    def put(ref, slot, value):
        high, low = split(value)
        ref[slot, 0:16, :] = high
        ref[slot, 16:32, :] = low

    constants = sweep_constants()

    def sweep(turn):
        keep, push = constants[turn]
        old_fine = source if turn == 0 else fine_e
        old_mid = mid_g if turn == 0 else mid_e
        old_fine_d = source if turn == 0 else fine_d
        old_mid_d = mid_g if turn == 0 else mid_d
        for r in range(4):
            put(fine_x, r, old_fine[r])
        for r in range(2):
            put(mid_x, r, old_mid[r])
        wait_halo(turn)
        for side in range(2):
            for row in range(2):
                put(fine_x, 4 + 2 * side + row, halo_in[turn, side, row])
            put(mid_x, 2 + side, halo_in[turn, side, 2])
        for r in range(4):
            left = jnp.concatenate([fine_x[fine_cols[r, k]] for k in range(8)], axis=1)
            applied = old_fine[r] + product(left, fine_w[r])
            step = keep * old_fine_d[r] + push * (source[r] - applied)
            fine_d[r] = step
            fine_e[r] = old_fine[r] + step
        for r in range(2):
            left = jnp.concatenate([mid_x[mid_cols[r, k]] for k in range(8)], axis=1)
            applied = old_mid[r] + product(left, mid_w[r])
            step = keep * old_mid_d[r] + push * (mid_g[r] - applied)
            mid_d[r] = step
            mid_e[r] = old_mid[r] + step
        if turn < 2:
            fill_halo(turn + 1, fine_e, mid_e)
            start_halo(turn + 1)

    sweep(0)

    @pl.when(centre)
    def _():
        wait_for(raw_in.at[:, pl.ds(0, 5)], raw_recv)
        rows = lax.broadcasted_iota(jnp.int32, (32, 8, 128), 1)
        cols = lax.broadcasted_iota(jnp.int32, (32, 8, 128), 2)
        value = raw_in[...]
        first = jnp.broadcast_to(value[:, 4:5, :], (32, 8, 128))
        second = pltpu.roll(first, 64, 2)
        picks = jnp.where(rows < 2, first, second)
        wanted = (rows < 4) & (cols // 8 == rows % 2)
        picks = jnp.where(wanted, picks, 0.0).reshape(256, 128).astype(BF16)
        high, low = split(value.reshape(256, 128))
        both = jnp.concatenate([high, low], axis=1)
        full = lax.dot_general(picks, both, (((0,), (0,)), ((), ())), preferred_element_type=F32)
        total = full[:16, :128] + full[:16, 128:]
        res_out[...] = total

        for step in (4, 3, 5, 2, 6, 1, 7):
            to_level = half * 8 + (mine + step) % 8
            remote(res_out, res_in.at[mine], res_send, res_recv, to_level, dom).start()
        pltpu.make_async_copy(res_out, res_in.at[mine], res_recv).start()


    @pl.when(centre)
    def _():
        wait_for(inv_in, inv_recv)
        for h in range(2):
            high, low = split(inv_in[h])
            inv_w[64 * h : 64 * h + 64, :] = high
            inv_w[128 + 64 * h : 192 + 64 * h, :] = low
        wait_for(res_in, res_recv)
        parts = []
        for c in range(8):
            block = jnp.concatenate([res_in[:, c, :], res_in[:, 8 + c, :]], axis=0)
            high, low = split(block)
            parts.append(jnp.concatenate([high, low], axis=0))
        left = jnp.concatenate(parts, axis=1)
        corr = product(left, inv_w[...])
        for peer in range(8):
            corr_out[peer, 0:1, :] = corr[peer : peer + 1, :]
            corr_out[peer, 1:2, :] = corr[8 + peer : 9 + peer, :]
        row = jnp.where(core == 0, half, 1 - half) * 4 + y_pos

        slot = final.at[x_pos, z_two, row]

        def result_to(peer, other_z):
            return remote(
                corr_out.at[peer],
                slot,
                z_send,
                z_recv.at[z_two],
                half * 8 + peer,
                other_z * 4 + x_pos,
            )

        peers = [(mine + step) % 8 for step in (4, 5, 3, 2, 6, 1, 7, 0)]

        @pl.when(half == 0)
        def _():
            for peer in peers:
                for step in (2, 1, 3, 0):
                    remote(
                        corr_out.at[peer],
                        slot,
                        early_send,
                        z_recv.at[z_two],
                        peer,
                        (x_pos + step) % 4,
                    ).start()

        @pl.when(half == 1)
        def _():
            for peer in peers:
                result_to(peer, 7).start()

        for first_half, second_half in ((1, 0), (2, 6), (7, 1), (6, 5), (5, 2)):
            for peer in peers:
                result_to(peer, jnp.where(half == 0, first_half, second_half)).start()
        for peer in peers:
            result_to(peer, 7 - z_pos).start()
        for peer in peers[:7]:
            result_to(peer, z_pos).start()
        pltpu.make_async_copy(corr_out.at[mine], slot, z_recv.at[z_two]).start()

    sweep(1)
    @pl.when(jnp.logical_not(early))
    def _():
        for which in range(2):
            wait_for(final.at[0, which], z_recv.at[which])
            for step in (2, 1, 3):
                remote(
                    final.at[x_pos, which],
                    final.at[x_pos, which],
                    x_send,
                    x_recv,
                    level,
                    z_pos * 4 + (x_pos + step) % 4,
                ).start()

    sweep(2)
    for i in range(4):
        partial[i] = DAMPING * (fine_e[i] + MID_WEIGHT * mid_e[fine_map[i]])

    @pl.when(early)
    def _():
        for which in range(2):
            wait_for(final.at[pl.ds(0, 2)], z_recv.at[which])

    @pl.when(jnp.logical_not(early))
    def _():
        wait_for(final.at[pl.ds(0, 3)], x_recv)

    for j in range(2):
        for n in range(8):
            first = 4 * (n // 2) + 2 * (n % 2)
            picked[first : first + 2, :] = final[n // 2, n % 2, mid_map[j]]
        joined[j] = (DAMPING * MID_WEIGHT * COARSE_WEIGHT * COARSE_WEIGHT) * picked[...]
    for i in range(4):
        out[i] = partial[i] + joined[fine_map[i]]

    for turn in range(3):

        @pl.when(has_low)
        def _():
            wait_for(halo_out.at[turn], halo_send.at[turn, 0])

        @pl.when(has_high)
        def _():
            wait_for(halo_out.at[turn], halo_send.at[turn, 1])

    @pl.when(jnp.logical_not(early))
    def _():
        wait_for(final.at[pl.ds(0, 3)], x_send)

    @pl.when(imports | (centre & (core == 1)))
    def _():
        wait_for(inverse_hbm, inv_send)

    @pl.when(jnp.logical_not(centre))
    def _():
        wait_for(raw_out, raw_send)

    @pl.when(centre)
    def _():
        wait_for(raw_out.at[pl.ds(0, 7)], raw_send)
        wait_for(res_in.at[pl.ds(0, 7)], res_send)
        @pl.when(half == 0)
        def _():
            wait_for(spare.at[pl.ds(0, 32)], early_send)
            wait_for(spare.at[pl.ds(0, 55)], z_send)

        @pl.when(half == 1)
        def _():
            wait_for(spare, z_send)


def shards(
    right_side,
    fine_blocks,
    fine_cols,
    fine_edges,
    mid_blocks,
    mid_cols,
    mid_edges,
    fine_map,
    mid_map,
    coarse_inverse,
):
    hbm = pl.BlockSpec(memory_space=pltpu.HBM)
    smem = pltpu.SMEM
    vmem = pltpu.VMEM
    dma = pltpu.SemaphoreType.DMA
    return pl.pallas_call(
        kernel,
        out_shape=jax.ShapeDtypeStruct(right_side.shape, F32),
        in_specs=[hbm] * 10,
        out_specs=pl.BlockSpec(memory_space=vmem),
        scratch_shapes=[
            smem((4, 8), jnp.int32),
            smem((2,), jnp.int32),
            smem((2, 8), jnp.int32),
            smem((1,), jnp.int32),
            smem((4,), jnp.int32),
            smem((2,), jnp.int32),
            vmem((4, 16, 128), F32),
            vmem((4, 8, 128, 128), F32),
            vmem((2, 8, 128, 128), F32),
            vmem((4, 256, 1024), BF16),
            vmem((2, 256, 1024), BF16),
            vmem((4, 16, 128), F32),
            vmem((4, 16, 128), F32),
            vmem((2, 16, 128), F32),
            vmem((2, 16, 128), F32),
            vmem((2, 16, 128), F32),
            vmem((8, 32, 128), BF16),
            vmem((4, 32, 128), BF16),
            vmem((3, 3, 16, 128), F32),
            vmem((3, 2, 3, 16, 128), F32),
            vmem((8, 5, 128), F32),
            vmem((32, 8, 128), F32),
            vmem((16, 128), F32),
            vmem((8, 16, 128), F32),
            vmem((2, 64, 1024), F32),
            vmem((256, 1024), BF16),
            vmem((8, 2, 128), F32),
            vmem((63, 2, 128), F32),
            vmem((4, 2, 8, 2, 128), F32),
            vmem((16, 128), F32),
            vmem((2, 16, 128), F32),
            vmem((4, 16, 128), F32),
            dma((13,)),
            dma((3, 2)),
            dma((3, 2)),
            dma,
            dma,
            dma,
            dma,
            dma,
            dma,
            dma,
            dma,
            dma((2,)),
            dma,
            dma,
        ],
        compiler_params=pltpu.CompilerParams(
            collective_id=0, has_side_effects=True, vmem_limit_bytes=40 * 1024 * 1024
        ),
    )(
        *[
            operand if operand is mid_edges else pltpu.with_memory_space_constraint(operand, pltpu.HBM)
            for operand in (
                fine_cols,
                fine_edges,
                mid_cols,
                mid_edges,
                fine_map,
                mid_map,
                right_side,
                fine_blocks,
                mid_blocks,
                coarse_inverse,
            )
        ]
    )


def solution(mesh):
    in_specs = (
        P("dom", "level", None),
        P("dom", None, None, None),
        P("dom", None),
        P("dom"),
        P("dom", None, None, None),
        P("dom", None),
        P("dom"),
        P("dom"),
        P("dom"),
        P("level", None),
    )
    out_specs = P("dom", "level", None)
    return jax.shard_map(shards, mesh=mesh, in_specs=in_specs, out_specs=out_specs, check_vma=False)
```

```python
import jax
import jax.numpy as jnp
from jax import lax
from jax.experimental import pallas as pl
from jax.experimental.pallas import tpu as pltpu
from jax.sharding import PartitionSpec as P

CAGG = 8
DEG = 4
CENTRE = 1.0
HALF_WIDTH = 0.7
DAMPING = 0.7
MID_WEIGHT = 0.5**0.5
COARSE_WEIGHT = CAGG**-0.5

F32 = jnp.float32
BF16 = jnp.bfloat16


def sweep_constants():
    ratio = CENTRE / HALF_WIDTH
    rho_prev = 1.0 / ratio
    constants = []
    for _ in range(DEG - 1):
        rho_next = 1.0 / (2.0 * ratio - rho_prev)
        constants.append((rho_next * rho_prev, 2.0 * rho_next / HALF_WIDTH))
        rho_prev = rho_next
    return constants


def split(value):
    high = value.astype(BF16)
    low = (value - high.astype(F32)).astype(BF16)
    return high, low


def product(left, right):
    full = lax.dot_general(left, right, (((1,), (1,)), ((), ())), preferred_element_type=F32)
    return full[:16, :128] + (full[:16, 128:] + full[16:, :128])


def wait_for(ref, sem):
    pltpu.make_async_copy(ref, ref, sem).wait()


def kernel(
    fine_cols_hbm,
    fine_edges_hbm,
    mid_cols_hbm,
    mid_edges_hbm,
    fine_map_hbm,
    mid_map_hbm,
    source_hbm,
    fine_hbm,
    mid_hbm,
    inverse_hbm,
    out,
    fine_cols,
    fine_edges,
    mid_cols,
    mid_edges,
    fine_map,
    mid_map,
    source,
    fine_raw,
    mid_raw,
    fine_w,
    mid_w,
    fine_e,
    fine_d,
    mid_g,
    mid_e,
    mid_d,
    fine_x,
    mid_x,
    halo_out,
    halo_in,
    raw_out,
    raw_in,
    res_out,
    res_in,
    inv_in,
    inv_w,
    corr_out,
    spare,
    final,
    picked,
    joined,
    partial,
    load_sem,
    halo_send,
    halo_recv,
    raw_send,
    raw_recv,
    inv_send,
    inv_recv,
    res_send,
    res_recv,
    z_send,
    early_send,
    z_recv,
    x_send,
    x_recv,
):
    level = lax.axis_index("level")
    dom = lax.axis_index("dom")
    half = level // 8
    mine = level % 8
    y_pos = mine // 2
    core = level % 2
    z_pos = dom // 4
    x_pos = dom % 4
    centre = (z_pos == 3) | (z_pos == 4)
    centre_i = jnp.where(centre, 1, 0)
    z_two = jnp.where(z_pos == 4, 1, 0)
    has_low = dom > 0
    has_high = dom < 31
    early = (half == 0) & (z_pos == 0)
    import_z = jnp.where(z_pos == 7, 3, 4)
    imports = (z_pos == 0) | (z_pos == 7)

    def remote(src, dst, send, recv, to_level, to_dom):
        return pltpu.make_async_remote_copy(
            src_ref=src,
            dst_ref=dst,
            send_sem=send,
            recv_sem=recv,
            device_id=(to_level, to_dom),
            device_id_type=pl.DeviceIdType.MESH,
        )

    barrier = pltpu.get_barrier_semaphore()

    def greet(to_level, to_dom):
        pl.semaphore_signal(
            barrier, inc=1, device_id=(to_level, to_dom), device_id_type=pl.DeviceIdType.MESH
        )

    @pl.when(centre)
    def _():
        for other_z in (7, 0, 6, 1, 5, 2, 4, 3):
            for other_x in range(4):

                @pl.when((z_pos != other_z) | (x_pos != other_x))
                def _():
                    greet(level, other_z * 4 + other_x)

        @pl.when(core == 0)
        def _():
            greet(level + 1, dom)

        @pl.when(core == 1)
        def _():
            from_dom = jnp.where(z_pos == 3, 7, 0) * 4 + x_pos
            greet((1 - half) * 8 + y_pos * 2, from_dom)
            greet((1 - half) * 8 + y_pos * 2 + 1, from_dom)

    load_small = [
        pltpu.make_async_copy(src, dst, load_sem.at[7 + n])
        for n, (src, dst) in enumerate(
            [
                (fine_map_hbm, fine_map),
                (mid_map_hbm, mid_map),
                (fine_edges_hbm, fine_edges),
                (mid_edges_hbm, mid_edges),
                (fine_cols_hbm, fine_cols),
                (mid_cols_hbm, mid_cols),
            ]
        )
    ]
    load_source = pltpu.make_async_copy(source_hbm, source, load_sem.at[0])
    for load in load_small[:2] + [load_source] + load_small[2:]:
        load.start()
    load_fine = [
        pltpu.make_async_copy(fine_hbm.at[r], fine_raw.at[r], load_sem.at[1 + r]) for r in range(4)
    ]
    load_mid = [
        pltpu.make_async_copy(mid_hbm.at[r], mid_raw.at[r], load_sem.at[5 + r]) for r in range(2)
    ]
    @pl.when(has_low)
    def _():
        greet(level, dom - 1)

    @pl.when(has_high)
    def _():
        greet(level, dom + 1)

    @pl.when(jnp.logical_not(early))
    def _():
        for step in range(1, 4):
            greet(level, z_pos * 4 + (x_pos + step) % 4)

    for other_z in (3, 4):
        for peer in range(8):

            @pl.when((z_pos != other_z) | (mine != peer))
            def _():
                greet(half * 8 + peer, other_z * 4 + x_pos)

    @pl.when(early)
    def _():
        for step in range(1, 4):
            for other_z in (3, 4):
                for peer in range(8):
                    greet(peer, other_z * 4 + (x_pos + step) % 4)

    for load in load_fine + load_mid:
        load.start()

    for load in load_small:
        load.wait()
    load_source.wait()
    lanes = lax.broadcasted_iota(jnp.int32, (1, 128), 1)
    for j in range(2):
        total = None
        for i in range(4):
            term = jnp.where(fine_map[i] == j, source[i], 0.0)
            total = term if total is None else total + term
        mid_g[j] = MID_WEIGHT * total
    wanted = jnp.where(lanes < 64, mid_map[0], mid_map[1])
    row = jnp.where((lanes % 64 < 16) & (lanes % 8 == wanted), 1.0, 0.0)
    for n in range(8):
        first = 4 * (n % 4) + 2 * (n // 4)
        for j in range(2):
            raw_out[n, 2 * j : 2 * j + 2, :] = mid_g[j, first : first + 2, :]
        raw_out[n, 4:5, :] = row

    def fill_halo(turn, fine_ref, mid_ref):
        halo_out[turn, 0] = fine_ref[fine_edges[0]]
        halo_out[turn, 1] = fine_ref[fine_edges[1]]
        halo_out[turn, 2] = mid_ref[mid_edges[0]]

    fill_halo(0, source, mid_g)

    @pl.when(dom == 0)
    def _():
        for turn in range(3):
            halo_in[turn, 0] = jnp.zeros((3, 16, 128), F32)

    @pl.when(dom == 31)
    def _():
        for turn in range(3):
            halo_in[turn, 1] = jnp.zeros((3, 16, 128), F32)

    @pl.when(centre)
    def _():
        raw_in[:, 5:8, :] = jnp.zeros((32, 3, 128), F32)

    sides = jnp.where(has_low, 1, 0) + jnp.where(has_high, 1, 0)
    waits = sides + 8 - centre_i + 3 + 63 * centre_i
    waits = waits + jnp.where(centre & (half == 0), 24, 0) - jnp.where(early, 3, 0)
    waits = waits + jnp.where(imports, 1, 0) + centre_i * core
    pl.semaphore_wait(barrier, waits)

    def halo_low(turn):
        return remote(
            halo_out.at[turn],
            halo_in.at[turn, 1],
            halo_send.at[turn, 0],
            halo_recv.at[turn, 1],
            level,
            dom - 1,
        )

    def halo_high(turn):
        return remote(
            halo_out.at[turn],
            halo_in.at[turn, 0],
            halo_send.at[turn, 1],
            halo_recv.at[turn, 0],
            level,
            dom + 1,
        )

    def start_halo(turn):
        @pl.when(has_low)
        def _():
            halo_low(turn).start()

        @pl.when(has_high)
        def _():
            halo_high(turn).start()

    def wait_halo(turn):
        @pl.when(has_low)
        def _():
            wait_for(halo_in.at[turn, 0], halo_recv.at[turn, 0])

        @pl.when(has_high)
        def _():
            wait_for(halo_in.at[turn, 1], halo_recv.at[turn, 1])

    raw_slot = raw_in.at[dom, pl.ds(0, 5)]
    far = jnp.where(z_pos < 4, 1, 0)
    for step, near in ((2, 0), (1, 0), (3, 0), (2, 1), (0, 0), (1, 1), (3, 1)):
        which = jnp.where(near == 1, 1 - far, far)
        to_x = (x_pos + step) % 4
        to_dom = (3 + which) * 4 + to_x
        remote(
            raw_out.at[which * 4 + to_x], raw_slot, raw_send, raw_recv, level, to_dom
        ).start()
    last = raw_out.at[(1 - far) * 4 + x_pos]

    @pl.when(jnp.logical_not(centre))
    def _():
        remote(last, raw_slot, raw_send, raw_recv, level, (4 - far) * 4 + x_pos).start()

    @pl.when(centre)
    def _():
        pltpu.make_async_copy(last, raw_slot, raw_recv).start()

    start_halo(0)

    @pl.when(centre & (core == 0))
    def _():
        pltpu.make_async_copy(inverse_hbm, inv_in.at[0], inv_recv).start()

    @pl.when(centre & (core == 1))
    def _():
        remote(inverse_hbm, inv_in.at[1], inv_send, inv_recv, level - 1, dom).start()

    @pl.when(imports)
    def _():
        remote(
            inverse_hbm,
            inv_in.at[core],
            inv_send,
            inv_recv,
            (1 - half) * 8 + y_pos * 2 + 1,
            import_z * 4 + x_pos,
        ).start()

    for r in range(4):
        load_fine[r].wait()
        for k in range(8):
            high, low = split(fine_raw[r, k])
            fine_w[r, 0:128, k * 128 : k * 128 + 128] = high
            fine_w[r, 128:256, k * 128 : k * 128 + 128] = low
    for r in range(2):
        load_mid[r].wait()
        for k in range(8):
            high, low = split(mid_raw[r, k])
            mid_w[r, 0:128, k * 128 : k * 128 + 128] = high
            mid_w[r, 128:256, k * 128 : k * 128 + 128] = low

    def put(ref, slot, value):
        high, low = split(value)
        ref[slot, 0:16, :] = high
        ref[slot, 16:32, :] = low

    constants = sweep_constants()

    def sweep(turn):
        keep, push = constants[turn]
        old_fine = source if turn == 0 else fine_e
        old_mid = mid_g if turn == 0 else mid_e
        old_fine_d = source if turn == 0 else fine_d
        old_mid_d = mid_g if turn == 0 else mid_d
        for r in range(4):
            put(fine_x, r, old_fine[r])
        for r in range(2):
            put(mid_x, r, old_mid[r])
        wait_halo(turn)
        for side in range(2):
            for row in range(2):
                put(fine_x, 4 + 2 * side + row, halo_in[turn, side, row])
            put(mid_x, 2 + side, halo_in[turn, side, 2])
        for r in range(4):
            left = jnp.concatenate([fine_x[fine_cols[r, k]] for k in range(8)], axis=1)
            applied = old_fine[r] + product(left, fine_w[r])
            step = keep * old_fine_d[r] + push * (source[r] - applied)
            fine_d[r] = step
            fine_e[r] = old_fine[r] + step
        for r in range(2):
            left = jnp.concatenate([mid_x[mid_cols[r, k]] for k in range(8)], axis=1)
            applied = old_mid[r] + product(left, mid_w[r])
            step = keep * old_mid_d[r] + push * (mid_g[r] - applied)
            mid_d[r] = step
            mid_e[r] = old_mid[r] + step
        if turn < 2:
            fill_halo(turn + 1, fine_e, mid_e)
            start_halo(turn + 1)

    sweep(0)

    @pl.when(centre)
    def _():
        wait_for(raw_in.at[:, pl.ds(0, 5)], raw_recv)
        rows = lax.broadcasted_iota(jnp.int32, (32, 8, 128), 1)
        cols = lax.broadcasted_iota(jnp.int32, (32, 8, 128), 2)
        value = raw_in[...]
        first = jnp.broadcast_to(value[:, 4:5, :], (32, 8, 128))
        second = pltpu.roll(first, 64, 2)
        picks = jnp.where(rows < 2, first, second)
        wanted = (rows < 4) & (cols // 8 == rows % 2)
        picks = jnp.where(wanted, picks, 0.0).reshape(256, 128).astype(BF16)
        high, low = split(value.reshape(256, 128))
        both = jnp.concatenate([high, low], axis=1)
        full = lax.dot_general(picks, both, (((0,), (0,)), ((), ())), preferred_element_type=F32)
        total = full[:16, :128] + full[:16, 128:]
        res_out[...] = total

        for step in (4, 3, 5, 2, 6, 1, 7):
            to_level = half * 8 + (mine + step) % 8
            remote(res_out, res_in.at[mine], res_send, res_recv, to_level, dom).start()
        pltpu.make_async_copy(res_out, res_in.at[mine], res_recv).start()


    @pl.when(centre)
    def _():
        wait_for(inv_in, inv_recv)
        for h in range(2):
            high, low = split(inv_in[h])
            inv_w[64 * h : 64 * h + 64, :] = high
            inv_w[128 + 64 * h : 192 + 64 * h, :] = low
        wait_for(res_in, res_recv)
        parts = []
        for c in range(8):
            block = jnp.concatenate([res_in[:, c, :], res_in[:, 8 + c, :]], axis=0)
            high, low = split(block)
            parts.append(jnp.concatenate([high, low], axis=0))
        left = jnp.concatenate(parts, axis=1)
        corr = product(left, inv_w[...])
        for peer in range(8):
            corr_out[peer, 0:1, :] = corr[peer : peer + 1, :]
            corr_out[peer, 1:2, :] = corr[8 + peer : 9 + peer, :]
        row = jnp.where(core == 0, half, 1 - half) * 4 + y_pos

        slot = final.at[x_pos, z_two, row]

        def result_to(peer, other_z):
            return remote(
                corr_out.at[peer],
                slot,
                z_send,
                z_recv.at[z_two],
                half * 8 + peer,
                other_z * 4 + x_pos,
            )

        peers = [(mine + step) % 8 for step in (4, 5, 3, 2, 6, 1, 7, 0)]

        for peer in peers:
            result_to(peer, jnp.where(half == 0, 1, 7)).start()

        @pl.when(half == 0)
        def _():
            for peer in peers:
                for step in (2, 1, 3, 0):
                    remote(
                        corr_out.at[peer],
                        slot,
                        early_send,
                        z_recv.at[z_two],
                        peer,
                        (x_pos + step) % 4,
                    ).start()

        @pl.when(half == 1)
        def _():
            for peer in peers:
                result_to(peer, 0).start()

        for first_half, second_half in ((2, 6), (7, 1), (6, 5), (5, 2)):
            for peer in peers:
                result_to(peer, jnp.where(half == 0, first_half, second_half)).start()
        for peer in peers:
            result_to(peer, 7 - z_pos).start()
        for peer in peers[:7]:
            result_to(peer, z_pos).start()
        pltpu.make_async_copy(corr_out.at[mine], slot, z_recv.at[z_two]).start()

    sweep(1)
    @pl.when(jnp.logical_not(early))
    def _():
        for which in range(2):
            wait_for(final.at[0, which], z_recv.at[which])
            for step in (2, 1, 3):
                remote(
                    final.at[x_pos, which],
                    final.at[x_pos, which],
                    x_send,
                    x_recv,
                    level,
                    z_pos * 4 + (x_pos + step) % 4,
                ).start()

    sweep(2)
    for i in range(4):
        partial[i] = DAMPING * (fine_e[i] + MID_WEIGHT * mid_e[fine_map[i]])

    @pl.when(early)
    def _():
        for which in range(2):
            wait_for(final.at[pl.ds(0, 2)], z_recv.at[which])

    @pl.when(jnp.logical_not(early))
    def _():
        wait_for(final.at[pl.ds(0, 3)], x_recv)

    for j in range(2):
        for n in range(8):
            first = 4 * (n // 2) + 2 * (n % 2)
            picked[first : first + 2, :] = final[n // 2, n % 2, mid_map[j]]
        joined[j] = (DAMPING * MID_WEIGHT * COARSE_WEIGHT * COARSE_WEIGHT) * picked[...]
    for i in range(4):
        out[i] = partial[i] + joined[fine_map[i]]

    for turn in range(3):

        @pl.when(has_low)
        def _():
            wait_for(halo_out.at[turn], halo_send.at[turn, 0])

        @pl.when(has_high)
        def _():
            wait_for(halo_out.at[turn], halo_send.at[turn, 1])

    @pl.when(jnp.logical_not(early))
    def _():
        wait_for(final.at[pl.ds(0, 3)], x_send)

    @pl.when(imports | (centre & (core == 1)))
    def _():
        wait_for(inverse_hbm, inv_send)

    @pl.when(jnp.logical_not(centre))
    def _():
        wait_for(raw_out, raw_send)

    @pl.when(centre)
    def _():
        wait_for(raw_out.at[pl.ds(0, 7)], raw_send)
        wait_for(res_in.at[pl.ds(0, 7)], res_send)
        @pl.when(half == 0)
        def _():
            wait_for(spare.at[pl.ds(0, 32)], early_send)
            wait_for(spare.at[pl.ds(0, 55)], z_send)

        @pl.when(half == 1)
        def _():
            wait_for(spare, z_send)


def shards(
    right_side,
    fine_blocks,
    fine_cols,
    fine_edges,
    mid_blocks,
    mid_cols,
    mid_edges,
    fine_map,
    mid_map,
    coarse_inverse,
):
    hbm = pl.BlockSpec(memory_space=pltpu.HBM)
    smem = pltpu.SMEM
    vmem = pltpu.VMEM
    dma = pltpu.SemaphoreType.DMA
    return pl.pallas_call(
        kernel,
        out_shape=jax.ShapeDtypeStruct(right_side.shape, F32),
        in_specs=[hbm] * 10,
        out_specs=pl.BlockSpec(memory_space=vmem),
        scratch_shapes=[
            smem((4, 8), jnp.int32),
            smem((2,), jnp.int32),
            smem((2, 8), jnp.int32),
            smem((1,), jnp.int32),
            smem((4,), jnp.int32),
            smem((2,), jnp.int32),
            vmem((4, 16, 128), F32),
            vmem((4, 8, 128, 128), F32),
            vmem((2, 8, 128, 128), F32),
            vmem((4, 256, 1024), BF16),
            vmem((2, 256, 1024), BF16),
            vmem((4, 16, 128), F32),
            vmem((4, 16, 128), F32),
            vmem((2, 16, 128), F32),
            vmem((2, 16, 128), F32),
            vmem((2, 16, 128), F32),
            vmem((8, 32, 128), BF16),
            vmem((4, 32, 128), BF16),
            vmem((3, 3, 16, 128), F32),
            vmem((3, 2, 3, 16, 128), F32),
            vmem((8, 5, 128), F32),
            vmem((32, 8, 128), F32),
            vmem((16, 128), F32),
            vmem((8, 16, 128), F32),
            vmem((2, 64, 1024), F32),
            vmem((256, 1024), BF16),
            vmem((8, 2, 128), F32),
            vmem((63, 2, 128), F32),
            vmem((4, 2, 8, 2, 128), F32),
            vmem((16, 128), F32),
            vmem((2, 16, 128), F32),
            vmem((4, 16, 128), F32),
            dma((13,)),
            dma((3, 2)),
            dma((3, 2)),
            dma,
            dma,
            dma,
            dma,
            dma,
            dma,
            dma,
            dma,
            dma((2,)),
            dma,
            dma,
        ],
        compiler_params=pltpu.CompilerParams(
            collective_id=0, has_side_effects=True, vmem_limit_bytes=40 * 1024 * 1024
        ),
    )(
        *[
            operand if operand is mid_edges else pltpu.with_memory_space_constraint(operand, pltpu.HBM)
            for operand in (
                fine_cols,
                fine_edges,
                mid_cols,
                mid_edges,
                fine_map,
                mid_map,
                right_side,
                fine_blocks,
                mid_blocks,
                coarse_inverse,
            )
        ]
    )


def solution(mesh):
    in_specs = (
        P("dom", "level", None),
        P("dom", None, None, None),
        P("dom", None),
        P("dom"),
        P("dom", None, None, None),
        P("dom", None),
        P("dom"),
        P("dom"),
        P("dom"),
        P("level", None),
    )
    out_specs = P("dom", "level", None)
    return jax.shard_map(shards, mesh=mesh, in_specs=in_specs, out_specs=out_specs, check_vma=False)
```
